32 devices in a mesh: groups: 2 (over y), row: 2 (over x), col: 8 (over z, core).
Axes of the slice: x: 2, y: 2, z: 4, core: 2. Of those that a mesh axis runs over, the one named last changes fastest.
Arguments:
- node_states: bfloat16 [4096, 1024], P(('groups', 'col')), parts along dimension 0, may hold values from -14 to 14
- query_weight: bfloat16 [1024, 1024], P(None, 'row'), may hold values from -1 to 1
- key_weight: bfloat16 [1024, 1024], P(None, 'row'), may hold values from -1 to 1
- value_weight: bfloat16 [1024, 1024], P(None, 'row'), may hold values from -0.1875 to 0.1875
- output_grad: bfloat16 [4096, 1024], P(('groups', 'col'), 'row'), parts along dimension 0, may hold values from -6 to 6
- pair_list: int32 [16, 32, 2], P(('groups', 'col')), parts along dimension 0, may hold values from 0 to 15, as said below
- pair_count: int32 [16], P(('groups', 'col')), parts along dimension 0, may hold values from 2 to 32, as said below
Outputs:
- attended: bfloat16 [4096, 1024], P(('groups', 'col'), 'row'), parts along dimension 0
- node_grad: float32 [4096, 1024], P(('groups', 'col'), 'row'), parts along dimension 0
- query_grad: float32 [2048, 1024], P(('groups', 'col'), 'row'), parts along dimension 0
- key_grad: float32 [2048, 1024], P(('groups', 'col'), 'row'), parts along dimension 0
- value_grad: float32 [2048, 1024], P(('groups', 'col'), 'row'), parts along dimension 0
The draws below stay inside these ranges and needn't reach their ends.
There are 2 independent parts, one for each index of `groups`. The reference program is written for one: setup_inputs(seed, part) draws one part's arguments, and reference() takes and returns one part's arrays. A program takes and returns all parts, laid end to end along the dimension named above; an argument that names none is the same for every part. Nothing has to cross between parts.
Inputs may be any that keep to these rules, and one draw needn't show every extreme that they name: `pair_list`: slot p of panel c holds a query block of the panel and a key block; the first pair_count[c] slots of a panel are distinct pairs and include (q, c * 2 + q) for every query block q; later slots hold valid indices and are not listed. `pair_count`: some panel lists all 32 slots.
All inputs are finite; a program needn't handle non-finite values.
Results may differ from the reference program's by a relative error of at most 0.015.
The reference program's roundings to bfloat16 on the way count: a program that leaves them out, or rounds other values in their place, can miss the bound.
Values may be sent and summed in bfloat16 or wider, within the bound.
A program may use at most 192 MiB of HBM per device.

```python
import math
import jax
import jax.numpy as jnp
from jax import lax

D = 1024
H = 16
DH = 64
BLK = 128
NB_DEV = 2
PAIRS = 32
NBLK = 16
NODES = 2048
HEAD_COLS = 512
N_ROW = 2
N_COL = 8


def draw_node_states(key, part):
    key_base = jax.random.fold_in(key, 0)
    return jnp.clip(jax.random.normal(key_base, (NODES, D), jnp.float32), -6.0, 6.0).astype(jnp.bfloat16)


def weight_pair(key):
    first_matrix = jax.random.normal(jax.random.fold_in(key, 101), (D, D), jnp.float32)
    second_matrix = jax.random.normal(jax.random.fold_in(key, 202), (D, D), jnp.float32)
    return (jnp.clip(first_matrix, -5.0, 5.0) / math.sqrt(D), jnp.clip(second_matrix, -5.0, 5.0) / math.sqrt(D))


def draw_query_weight(key, part):
    return weight_pair(key)[0].astype(jnp.bfloat16)


def draw_key_weight(key, part):
    first_matrix, second_matrix = weight_pair(key)
    return second_matrix.astype(jnp.bfloat16)


def lists_and_counts(key):
    folded = jax.random.fold_in(key, 7)
    key_perm, key_level, key_peak = jax.random.split(folded, 3)
    panel_total = NBLK // NB_DEV
    candidates = NB_DEV * NBLK
    panel_range = jnp.arange(panel_total, dtype=jnp.int32)

    def one_panel(panel_key, panel):
        shuffled = jax.random.permutation(panel_key, candidates).astype(jnp.int32)
        query_block = shuffled // NBLK
        key_block = shuffled % NBLK
        own_block = key_block == panel * NB_DEV + query_block
        ranking = jnp.argsort(jnp.where(own_block, 0, 1).astype(jnp.int32), stable=True)
        chosen = shuffled[ranking][:PAIRS]
        return jnp.stack([chosen // NBLK, chosen % NBLK], axis=1)
    panel_keys = jax.random.split(key_perm, panel_total)
    pair_lists = jax.vmap(one_panel)(panel_keys, panel_range)
    level_draw = jax.random.randint(key_level, (panel_total,), 0, 1001)
    extra_pairs = (PAIRS - NB_DEV) * level_draw * level_draw // 1000000
    peak_panel = jax.random.randint(key_peak, (), 0, panel_total)
    pair_counts = jnp.where(panel_range == peak_panel, PAIRS, NB_DEV + extra_pairs)
    return (pair_lists.astype(jnp.int32), pair_counts.astype(jnp.int32))


def draw_pair_list(key, part):
    return lists_and_counts(key)[0]


def draw_pair_count(key, part):
    return lists_and_counts(key)[1]


def levels(stream_key, shape, shards, least, largest):
    def one(position, shards_of):
        steps = jax.random.uniform(jax.random.fold_in(jax.random.fold_in(stream_key, 6), position), (shards_of,), jnp.float32, least / len(shards), largest / len(shards))
        return jnp.repeat(jnp.exp(steps), shape[position] // shards_of).reshape((-1,) + (1,) * (len(shape) - position - 1))

    gain = one(*shards[0])
    for cut in shards[1:]:
        gain = gain * one(*cut)
    return gain


def centred(rng, shape, scale, most, pieces=(), kind=jnp.bfloat16):
    drawn = jax.random.normal(rng, shape, jnp.float32) * scale
    if len(pieces) > 0:
        drawn = levels(rng, shape, pieces, -0.22, 0.18) * drawn
    return jnp.clip(drawn, min=-most, max=most).astype(kind)


def setup_inputs(seed: int = 0, part: int = 0) -> dict:
    splits = jax.random.split(jax.random.key(seed), 8)
    own_keys = jax.random.split(jax.random.fold_in(splits[7], part), 8)
    return {
        "node_states": draw_node_states(jax.random.fold_in(jax.random.fold_in(splits[7], part), 71), part),
        "query_weight": draw_query_weight(jax.random.fold_in(splits[7], 71), part),
        "key_weight": draw_key_weight(jax.random.fold_in(splits[7], 71), part),
        "value_weight": centred(splits[3], (D, D), D ** -0.5, 0.1875, ((1, 2),)),
        "output_grad": centred(own_keys[4], (NODES, D), 1.0, 6.0, ((0, 8), (1, 2))),
        "pair_list": draw_pair_list(jax.random.fold_in(jax.random.fold_in(splits[7], part), 71), part),
        "pair_count": draw_pair_count(jax.random.fold_in(jax.random.fold_in(splits[7], part), 71), part),
    }


def project(node_states, weight):
    return jnp.dot(node_states, weight, preferred_element_type=jnp.float32).astype(jnp.bfloat16)

def reference(node_states, query_weight, key_weight, value_weight, output_grad, pair_list, pair_count):
    factor = 1.0 / math.sqrt(DH)
    queries = project(node_states, query_weight)
    keys_all = project(node_states, key_weight)
    values_all = project(node_states, value_weight)
    query_panels = queries.reshape(N_COL, NB_DEV, BLK, H, DH)
    grad_panels = output_grad.reshape(N_COL, NB_DEV, BLK, H, DH)
    key_blocks = keys_all.reshape(NBLK, BLK, H, DH)
    value_blocks = values_all.reshape(NBLK, BLK, H, DH)
    slot_range = jnp.arange(PAIRS, dtype=jnp.int32)
    block_range = jnp.arange(NB_DEV, dtype=jnp.int32)

    def one_panel(state_pair, inputs):
        key_acc, value_acc = state_pair
        query_panel, grad_panel, pair_rows, pair_total = inputs
        query_block = pair_rows[:, 0].astype(jnp.int32)
        key_block = pair_rows[:, 1].astype(jnp.int32)
        slot_live = slot_range < pair_total
        owners = jnp.logical_and(query_block[:, None] == block_range[None, :], slot_live[:, None])
        owners_f = owners.astype(jnp.float32)
        query_pick = query_panel[query_block].astype(jnp.float32)
        key_pick = key_blocks[key_block].astype(jnp.float32)
        value_pick = value_blocks[key_block].astype(jnp.float32)
        grad_pick = grad_panel[query_block].astype(jnp.float32)
        scores = jnp.einsum('pihd,pjhd->phij', query_pick, key_pick) * factor
        pair_top = lax.optimization_barrier(jnp.max(scores, axis=3))
        block_top = lax.optimization_barrier(jnp.max(jnp.where(owners[:, :, None, None], pair_top[:, None], -jnp.inf), axis=0))
        shifted = jnp.where(slot_live[:, None, None, None], scores - block_top[query_block][..., None], -jnp.inf)
        exp_terms = jnp.exp(shifted)
        block_total = jnp.einsum('pn,phi->nhi', owners_f, lax.optimization_barrier(jnp.sum(exp_terms, axis=3)))
        weights = (exp_terms / block_total[query_block][..., None]).astype(jnp.bfloat16)
        weights_f = lax.optimization_barrier(weights).astype(jnp.float32)
        outputs = jnp.einsum('pn,pihd->nihd', owners_f, jnp.einsum('phij,pjhd->pihd', weights_f, value_pick))
        deltas = lax.optimization_barrier(jnp.sum(grad_panel.astype(jnp.float32) * outputs, axis=3))
        value_part = jnp.einsum('phij,pihd->pjhd', weights_f, grad_pick)
        prob_grad = jnp.einsum('pihd,pjhd->phij', grad_pick, value_pick)
        delta_pick = jnp.transpose(deltas[query_block], (0, 2, 1))
        score_grad = (weights_f * (prob_grad - delta_pick[..., None])).astype(jnp.bfloat16)
        score_grad = lax.optimization_barrier(score_grad).astype(jnp.float32)
        query_part = jnp.einsum('phij,pjhd->pihd', score_grad, key_pick) * factor
        key_part = jnp.einsum('phij,pihd->pjhd', score_grad, query_pick) * factor
        query_rows = jnp.einsum('pn,pihd->nihd', owners_f, query_part)
        key_sum = jax.ops.segment_sum(key_part, key_block, num_segments=NBLK)
        value_sum = jax.ops.segment_sum(value_part, key_block, num_segments=NBLK)
        key_acc = key_acc + lax.optimization_barrier(key_sum.astype(jnp.bfloat16)).astype(jnp.float32)
        value_acc = value_acc + lax.optimization_barrier(value_sum.astype(jnp.bfloat16)).astype(jnp.float32)
        return ((key_acc, value_acc), (outputs, query_rows))
    empty_sum = jnp.zeros((NBLK, BLK, H, DH), jnp.float32)
    (key_acc, value_acc), (outputs, query_rows) = lax.scan(one_panel, (empty_sum, empty_sum), (query_panels, grad_panels, pair_list, pair_count))
    attended = outputs.reshape(NODES, D).astype(jnp.bfloat16)
    query_rows_grad = query_rows.reshape(NODES, D).astype(jnp.bfloat16)
    key_rows_grad = key_acc.reshape(NODES, D).astype(jnp.bfloat16)
    value_rows_grad = value_acc.reshape(NODES, D).astype(jnp.bfloat16)
    contract = (((1,), (1,)), ((), ()))
    pairs_of = ((query_rows_grad, query_weight), (key_rows_grad, key_weight), (value_rows_grad, value_weight))

    def add_group(group_index, running):
        start = (group_index * HEAD_COLS).astype(jnp.int32)
        part = jnp.zeros((NODES, D), jnp.float32)
        for rows, weight in pairs_of:
            left = lax.dynamic_slice_in_dim(rows, start, HEAD_COLS, 1)
            right = lax.dynamic_slice_in_dim(weight, start, HEAD_COLS, 1)
            part = part + lax.dot_general(left, right, contract, preferred_element_type=jnp.float32)
        rounded = lax.optimization_barrier(part.astype(jnp.bfloat16)).astype(jnp.float32)
        return running + rounded
    node_grad = lax.fori_loop(0, N_ROW, add_group, jnp.zeros((NODES, D), jnp.float32))
    over_nodes = (((0,), (0,)), ((), ()))
    query_grad = lax.dot_general(node_states, query_rows_grad, over_nodes, preferred_element_type=jnp.float32)
    key_grad = lax.dot_general(node_states, key_rows_grad, over_nodes, preferred_element_type=jnp.float32)
    value_grad = lax.dot_general(node_states, value_rows_grad, over_nodes, preferred_element_type=jnp.float32)
    return (attended, node_grad, query_grad, key_grad, value_grad)
```

```python
import functools
import math

import jax
import jax.numpy as jnp
from jax import lax
from jax.experimental import pallas as pl
from jax.experimental.pallas import tpu as pltpu
from jax.sharding import PartitionSpec as P

DH = 64
BLK = 128


LOWEST = -1e30
EXACT = lax.Precision.HIGHEST


def slot_batch(pair_rows, pair_total, turn_index, width, blocks):
    start = turn_index * width
    query_block = pair_rows[:, 0]
    key_block = pair_rows[:, 1]
    slot_live = start + jnp.arange(width, dtype=jnp.int32) < pair_total
    owners = jnp.logical_and(
        query_block[:, None] == jnp.arange(blocks, dtype=jnp.int32)[None, :], slot_live[:, None]
    )
    return (query_block, key_block, slot_live, owners)


def batch_tiles(query_tiles, table_tiles, query_block, key_block, head_cols, factor):
    head_count = head_cols // DH
    width = query_block.shape[0]
    query_pick = jnp.take(query_tiles, query_block, axis=0)
    table_pick = jnp.take(table_tiles, key_block, axis=0)
    key_pick = table_pick[:, :, :head_cols].reshape(width, BLK, head_count, DH)
    value_pick = table_pick[:, :, head_cols:].reshape(width, BLK, head_count, DH)
    scores = (
        jnp.einsum("sihd,sjhd->shij", query_pick, key_pick, preferred_element_type=jnp.float32)
        * factor
    )
    return (query_pick, key_pick, value_pick, scores)


def batch_weights(scores, row_top, totals, query_block, slot_live):
    top_pick = jnp.take(row_top, query_block, axis=0)
    total_pick = jnp.take(totals, query_block, axis=0)
    weights = jnp.exp(scores - top_pick[..., None]) / total_pick[..., None]
    return jnp.where(slot_live[:, None, None, None], weights, 0.0).astype(jnp.bfloat16)


def per_device_slots(
    node_states, query_weight, key_weight, value_weight, output_grad, pair_list, pair_count
):
    head_cols = query_weight.shape[1]
    head_count = head_cols // DH
    panel_rows = node_states.shape[0]
    blocks = panel_rows // BLK
    factor = 1.0 / math.sqrt(DH)
    pair_rows = pair_list[0]
    pair_total = pair_count[0]
    width = math.gcd(pair_rows.shape[0], 32)
    turns = (pair_total + width - 1) // width
    queries = jnp.dot(node_states, query_weight, preferred_element_type=jnp.float32).astype(
        jnp.bfloat16
    )
    keys_here = jnp.dot(node_states, key_weight, preferred_element_type=jnp.float32).astype(
        jnp.bfloat16
    )
    values_here = jnp.dot(node_states, value_weight, preferred_element_type=jnp.float32).astype(
        jnp.bfloat16
    )
    local_table = jnp.concatenate([keys_here, values_here], axis=1)
    key_table = lax.all_gather(local_table, "col", axis=0, tiled=True)
    key_blocks_all = key_table.shape[0] // BLK
    query_tiles = queries.reshape(blocks, BLK, head_count, DH)
    table_tiles = key_table.reshape(key_blocks_all, BLK, 2 * head_cols)

    def stats_turn(turn_index, state_pair):
        row_top, totals = state_pair
        query_block, key_block, slot_live, owners = slot_batch(
            pair_rows, pair_total, turn_index, width, blocks
        )
        scores = batch_tiles(query_tiles, table_tiles, query_block, key_block, head_cols, factor)[3]
        pair_top = jnp.max(scores, axis=3)
        block_top = jnp.max(jnp.where(owners[:, :, None, None], pair_top[:, None], LOWEST), axis=0)
        new_top = jnp.maximum(row_top, block_top)
        top_pick = jnp.take(new_top, query_block, axis=0)
        exp_terms = jnp.where(
            slot_live[:, None, None, None], jnp.exp(scores - top_pick[..., None]), 0.0
        )
        added = jnp.einsum(
            "sn,shi->nhi", owners.astype(jnp.float32), jnp.sum(exp_terms, axis=3), precision=EXACT
        )
        totals = totals * jnp.exp(row_top - new_top) + added
        return (new_top, totals)

    start_top = jnp.full((blocks, head_count, BLK), LOWEST, jnp.float32)
    start_total = jnp.zeros((blocks, head_count, BLK), jnp.float32)
    row_top, totals = lax.fori_loop(0, turns, stats_turn, (start_top, start_total))

    def attend_turn(turn_index, output):
        query_block, key_block, slot_live, owners = slot_batch(
            pair_rows, pair_total, turn_index, width, blocks
        )
        query_pick, key_pick, value_pick, scores = batch_tiles(
            query_tiles, table_tiles, query_block, key_block, head_cols, factor
        )
        weights = batch_weights(scores, row_top, totals, query_block, slot_live)
        update = jnp.einsum(
            "shij,sjhd->sihd", weights, value_pick, preferred_element_type=jnp.float32
        )
        return output + jnp.einsum(
            "sn,sihd->nihd", owners.astype(jnp.float32), update, precision=EXACT
        )

    output = lax.fori_loop(
        0, turns, attend_turn, jnp.zeros((blocks, BLK, head_count, DH), jnp.float32)
    )
    attended = output.reshape(panel_rows, head_cols).astype(jnp.bfloat16)
    grad_tiles = output_grad.reshape(blocks, BLK, head_count, DH)
    deltas = jnp.sum(grad_tiles.astype(jnp.float32) * output, axis=3)
    back_table = lax.all_gather(local_table, "col", axis=0, tiled=True)
    back_tiles = back_table.reshape(key_blocks_all, BLK, 2 * head_cols)

    def backward_turn(turn_index, state_pair):
        grad_rows, key_grads = state_pair
        query_block, key_block, slot_live, owners = slot_batch(
            pair_rows, pair_total, turn_index, width, blocks
        )
        query_pick, key_pick, value_pick, scores = batch_tiles(
            query_tiles, back_tiles, query_block, key_block, head_cols, factor
        )
        weights = batch_weights(scores, row_top, totals, query_block, slot_live)
        grad_pick = jnp.take(grad_tiles, query_block, axis=0)
        value_part = jnp.einsum(
            "shij,sihd->sjhd", weights, grad_pick, preferred_element_type=jnp.float32
        )
        prob_grad = jnp.einsum(
            "sihd,sjhd->shij", grad_pick, value_pick, preferred_element_type=jnp.float32
        )
        delta_pick = jnp.transpose(jnp.take(deltas, query_block, axis=0), (0, 2, 1))
        score_grad = (weights.astype(jnp.float32) * (prob_grad - delta_pick[..., None])).astype(
            jnp.bfloat16
        )
        query_part = (
            jnp.einsum("shij,sjhd->sihd", score_grad, key_pick, preferred_element_type=jnp.float32)
            * factor
        )
        key_part = (
            jnp.einsum(
                "shij,sihd->sjhd", score_grad, query_pick, preferred_element_type=jnp.float32
            )
            * factor
        )
        grad_rows = grad_rows + jnp.einsum(
            "sn,sihd->nihd", owners.astype(jnp.float32), query_part, precision=EXACT
        )
        rows_update = jnp.concatenate(
            [key_part.reshape(width, BLK, head_cols), value_part.reshape(width, BLK, head_cols)],
            axis=2,
        )
        key_grads = key_grads + jax.ops.segment_sum(
            rows_update, key_block, num_segments=key_blocks_all
        )
        return (grad_rows, key_grads)

    start_rows = jnp.zeros((blocks, BLK, head_count, DH), jnp.float32)
    start_keys = jnp.zeros((key_blocks_all, BLK, 2 * head_cols), jnp.float32)
    grad_rows, key_grads = lax.fori_loop(0, turns, backward_turn, (start_rows, start_keys))
    key_grads = key_grads.reshape(key_blocks_all * BLK, 2 * head_cols)
    pair_grads = lax.psum_scatter(
        key_grads.astype(jnp.bfloat16), "col", scatter_dimension=0, tiled=True
    ).astype(jnp.float32)
    query_rows_grad = grad_rows.reshape(panel_rows, head_cols).astype(jnp.bfloat16)
    key_rows_grad = pair_grads[:, :head_cols].astype(jnp.bfloat16)
    value_rows_grad = pair_grads[:, head_cols:].astype(jnp.bfloat16)
    contract = (((1,), (1,)), ((), ()))
    partial_sum = lax.dot_general(
        query_rows_grad, query_weight, contract, preferred_element_type=jnp.float32
    )
    partial_sum = partial_sum + lax.dot_general(
        key_rows_grad, key_weight, contract, preferred_element_type=jnp.float32
    )
    partial_sum = partial_sum + lax.dot_general(
        value_rows_grad, value_weight, contract, preferred_element_type=jnp.float32
    )
    node_grad = lax.psum_scatter(
        partial_sum.astype(jnp.bfloat16), "row", scatter_dimension=1, tiled=True
    ).astype(jnp.float32)
    over_nodes = (((0,), (0,)), ((), ()))
    query_term = lax.dot_general(
        node_states, query_rows_grad, over_nodes, preferred_element_type=jnp.float32
    )
    key_term = lax.dot_general(
        node_states, key_rows_grad, over_nodes, preferred_element_type=jnp.float32
    )
    value_term = lax.dot_general(
        node_states, value_rows_grad, over_nodes, preferred_element_type=jnp.float32
    )
    query_grad, key_grad, value_grad = (
        lax.psum_scatter(
            query_term.astype(jnp.bfloat16), "col", scatter_dimension=0, tiled=True
        ).astype(jnp.float32),
        lax.psum_scatter(
            key_term.astype(jnp.bfloat16), "col", scatter_dimension=0, tiled=True
        ).astype(jnp.float32),
        lax.psum_scatter(
            value_term.astype(jnp.bfloat16), "col", scatter_dimension=0, tiled=True
        ).astype(jnp.float32),
    )
    return (attended, node_grad, query_grad, key_grad, value_grad)


MESH = pl.DeviceIdType.MESH
GROUP = 4


def meet(axes):
    barrier = pltpu.get_barrier_semaphore()
    total = 0
    for axis, count in axes:
        me = lax.axis_index(axis)
        for step in range(1, count):
            peer = lax.rem(me + step, count)
            pl.semaphore_signal(barrier, inc=1, device_id={axis: peer}, device_id_type=MESH)
            total += 1
    pl.semaphore_wait(barrier, total)


def spread_kernel(
    n, x_ref, wq_ref, wk_ref, wv_ref, grad_ref, code_ref, heads_ref, codes_ref,
    outbox, own_sem, send_sem, recv_sem, code_send, code_recv, code_own,
):
    me = lax.axis_index("col")
    meet([("col", n)])

    def code_copy(peer, slot):
        return pltpu.make_async_remote_copy(
            src_ref=code_ref, dst_ref=codes_ref.at[slot], send_sem=code_send.at[peer],
            recv_sem=code_recv.at[slot], device_id={"col": peer}, device_id_type=MESH,
        )

    def head_copy(peer, slot):
        return pltpu.make_async_remote_copy(
            src_ref=outbox.at[peer], dst_ref=heads_ref.at[slot], send_sem=send_sem.at[peer],
            recv_sem=recv_sem.at[slot], device_id={"col": peer}, device_id_type=MESH,
        )

    peers = [lax.rem(me + step, n) for step in range(1, n)]
    for peer in peers:
        code_copy(peer, me).start()
    own_code = pltpu.make_async_copy(code_ref, codes_ref.at[me], code_own)
    own_code.start()
    x = x_ref[...]
    factor = 1.0 / math.sqrt(DH)
    queries = jnp.dot(x, wq_ref[...], preferred_element_type=jnp.float32)
    queries = (queries.astype(jnp.bfloat16).astype(jnp.float32) * factor).astype(jnp.bfloat16)
    keys = jnp.dot(x, wk_ref[...], preferred_element_type=jnp.float32).astype(jnp.bfloat16)
    values = jnp.dot(x, wv_ref[...], preferred_element_type=jnp.float32).astype(jnp.bfloat16)
    grads = grad_ref[...]
    for head in range(n):
        cols = slice(head * DH, (head + 1) * DH)
        outbox[head] = jnp.concatenate(
            [queries[:, cols], grads[:, cols], keys[:, cols], values[:, cols]], axis=1
        )
    for peer in peers:
        head_copy(peer, me).start()
    own = pltpu.make_async_copy(outbox.at[me], heads_ref.at[me], own_sem)
    own.start()
    own.wait()
    own_code.wait()
    for peer in peers:
        code_copy(peer, peer).wait_recv()
        head_copy(peer, peer).wait_recv()
    for peer in peers:
        code_copy(peer, me).wait_send()
        head_copy(peer, me).wait_send()


def spread(node_states, query_weight, key_weight, value_weight, output_grad, codes, n):
    rows = node_states.shape[0]
    width = 4 * DH
    vmem = pl.BlockSpec(memory_space=pltpu.VMEM)
    return pl.pallas_call(
        functools.partial(spread_kernel, n),
        out_shape=(
            jax.ShapeDtypeStruct((n, rows, width), jnp.bfloat16),
            jax.ShapeDtypeStruct((n,) + codes.shape, jnp.int32),
        ),
        in_specs=[vmem] * 6,
        out_specs=(pl.BlockSpec(memory_space=pl.ANY), pl.BlockSpec(memory_space=pl.ANY)),
        scratch_shapes=[
            pltpu.VMEM((n, rows, width), jnp.bfloat16),
            pltpu.SemaphoreType.DMA,
            pltpu.SemaphoreType.DMA((n,)),
            pltpu.SemaphoreType.DMA((n,)),
            pltpu.SemaphoreType.DMA((n,)),
            pltpu.SemaphoreType.DMA((n,)),
            pltpu.SemaphoreType.DMA,
        ],
        compiler_params=pltpu.CompilerParams(
            collective_id=0, has_side_effects=True, vmem_limit_bytes=24 << 20
        ),
        cost_estimate=pl.CostEstimate(
            flops=6 * rows * node_states.shape[1] * n * DH, bytes_accessed=40 << 20, transcendentals=0
        ),
        name="spread_heads",
    )(node_states, query_weight, key_weight, value_weight, output_grad, codes)


def attend_kernel(
    n, blocks, codes_ref, heads_ref, out_ref, pairs_acc, scores_buf, grads_buf, found, counts
):
    lanes = lax.broadcasted_iota(jnp.int32, (BLK, 2 * DH), 1)
    first = lanes < DH
    key_total = n * blocks
    nt = (((1,), (1,)), ((), ()))
    pairs_acc[...] = jnp.zeros_like(pairs_acc)

    def collect(panel):
        for q in range(blocks):
            counts[q] = 0
            for k in range(key_total):
                found[q, k] = 0
        total = codes_ref[panel, 2, 0]

        def one(slot, carry):
            q = codes_ref[panel, 0, slot]
            place = counts[q]
            found[q, place] = codes_ref[panel, 1, slot]
            counts[q] = place + 1
            return carry

        lax.fori_loop(0, total, one, 0)

    def work(panel, groups):
        width = GROUP * BLK
        stacks = []
        for q in range(blocks):
            both = heads_ref[panel, q * BLK : (q + 1) * BLK, : 2 * DH]
            zero = jnp.zeros_like(both)
            stacks.append(
                jnp.concatenate([jnp.where(first, both, zero), jnp.where(first, zero, both)], axis=0)
            )

        def table(q, g):
            parts = []
            for j in range(GROUP):
                k = found[q, g * GROUP + j]
                start = pl.multiple_of(lax.rem(k, blocks) * BLK, BLK)
                parts.append(heads_ref[lax.div(k, blocks), pl.ds(start, BLK), 2 * DH :])
            return jnp.concatenate(parts, axis=0)

        tops, totals, outs, deltas = [], [], [], []
        for q in range(blocks):
            top = jnp.full((BLK, BLK), LOWEST, jnp.float32)
            for g in range(groups):
                both = lax.dot_general(stacks[q], table(q, g), nt, preferred_element_type=jnp.float32)
                grads_buf[q, g] = both[BLK:]
                for j in range(GROUP):
                    tile = both[:BLK, j * BLK : (j + 1) * BLK]
                    live = g * GROUP + j < counts[q]
                    tile = jnp.where(live, tile, LOWEST)
                    scores_buf[q, g, :, j * BLK : (j + 1) * BLK] = tile
                    top = jnp.maximum(top, tile)
            tops.append(jnp.max(top, axis=1, keepdims=True))
        for q in range(blocks):
            total = jnp.zeros((BLK, BLK), jnp.float32)
            for g in range(groups):
                terms = jnp.exp(scores_buf[q, g] - tops[q])
                scores_buf[q, g] = terms
                for j in range(GROUP):
                    total = total + terms[:, j * BLK : (j + 1) * BLK]
            totals.append(1.0 / jnp.sum(total, axis=1, keepdims=True))
        for q in range(blocks):
            out = jnp.zeros((BLK, 2 * DH), jnp.float32)
            for g in range(groups):
                weights = (scores_buf[q, g] * totals[q]).astype(jnp.bfloat16)
                out = out + jnp.dot(weights, table(q, g), preferred_element_type=jnp.float32)
            outs.append(out)
            grad = stacks[q][BLK:].astype(jnp.float32)
            deltas.append(jnp.sum(grad * out, axis=1, keepdims=True))
        for q in range(blocks):
            rows_grad = jnp.zeros((BLK, 2 * DH), jnp.float32)
            turned = stacks[q].T
            for g in range(groups):
                weights = (scores_buf[q, g] * totals[q]).astype(jnp.bfloat16)
                score_grad = (
                    weights.astype(jnp.float32) * (grads_buf[q, g] - deltas[q])
                ).astype(jnp.bfloat16)
                rows_grad = rows_grad + jnp.dot(
                    score_grad, table(q, g), preferred_element_type=jnp.float32
                )
                pair = jnp.dot(
                    turned,
                    jnp.concatenate([score_grad, weights], axis=0),
                    preferred_element_type=jnp.float32,
                )
                for j in range(GROUP):
                    k = found[q, g * GROUP + j]
                    pairs_acc[k] = pairs_acc[k] + pair[:, j * BLK : (j + 1) * BLK]
            factor = 1.0 / math.sqrt(DH)
            out_ref[panel, q * BLK : (q + 1) * BLK, : 2 * DH] = jnp.where(
                first, rows_grad * factor, outs[q]
            ).astype(jnp.bfloat16)

    def one_panel(panel, carry):
        collect(panel)
        most = counts[0]
        for q in range(1, blocks):
            most = jnp.maximum(most, counts[q])
        groups = lax.div(most + (GROUP - 1), GROUP)
        for size in range(1, key_total // GROUP + 1):
            pl.when(groups == size)(functools.partial(work, panel, size))
        return carry

    lax.fori_loop(0, n, one_panel, 0)
    for k in range(key_total):
        row = (k % blocks) * BLK
        out_ref[k // blocks, row : row + BLK, 2 * DH :] = pairs_acc[k].T.astype(jnp.bfloat16)


def attend(heads, codes, n, blocks):
    key_total = n * blocks
    groups = key_total // GROUP
    tiles = key_total * key_total
    return pl.pallas_call(
        functools.partial(attend_kernel, n, blocks),
        out_shape=jax.ShapeDtypeStruct(heads.shape, jnp.bfloat16),
        in_specs=[
            pl.BlockSpec(memory_space=pltpu.SMEM),
            pl.BlockSpec(memory_space=pltpu.VMEM),
        ],
        out_specs=pl.BlockSpec(memory_space=pltpu.VMEM),
        scratch_shapes=[
            pltpu.VMEM((key_total, 2 * DH, BLK), jnp.float32),
            pltpu.VMEM((blocks, groups, BLK, GROUP * BLK), jnp.float32),
            pltpu.VMEM((blocks, groups, BLK, GROUP * BLK), jnp.float32),
            pltpu.SMEM((blocks, key_total), jnp.int32),
            pltpu.SMEM((blocks,), jnp.int32),
        ],
        compiler_params=pltpu.CompilerParams(vmem_limit_bytes=24 << 20),
        cost_estimate=pl.CostEstimate(
            flops=tiles * 24 * BLK * BLK * DH, bytes_accessed=80 << 20,
            transcendentals=tiles * BLK * BLK,
        ),
        name="attend_heads",
    )(codes, heads)


def collect_kernel(
    n, n_row, res_ref, x_ref, wq_ref, wk_ref, wv_ref,
    att_ref, node_ref, qg_ref, kg_ref, vg_ref,
    inbox, terms_out, terms_in, part_out, part_in,
    send_sem, recv_sem, term_send, term_recv, row_send, row_recv,
):
    me = lax.axis_index("col")
    my_row = lax.axis_index("row")
    meet([("col", n), ("row", n_row)])
    peers = [lax.rem(me + step, n) for step in range(1, n)]
    row_peers = [lax.rem(my_row + step, n_row) for step in range(1, n_row)]
    cols = part_out.shape[2]

    def res_copy(peer, slot):
        return pltpu.make_async_remote_copy(
            src_ref=res_ref.at[peer], dst_ref=inbox.at[slot], send_sem=send_sem.at[peer],
            recv_sem=recv_sem.at[slot], device_id={"col": peer}, device_id_type=MESH,
        )

    def term_copy(peer, slot):
        return pltpu.make_async_remote_copy(
            src_ref=terms_out.at[peer], dst_ref=terms_in.at[slot], send_sem=term_send.at[peer],
            recv_sem=term_recv.at[slot], device_id={"col": peer}, device_id_type=MESH,
        )

    def row_copy(peer, slot):
        return pltpu.make_async_remote_copy(
            src_ref=part_out.at[peer], dst_ref=part_in.at[slot], send_sem=row_send.at[peer],
            recv_sem=row_recv.at[slot], device_id={"row": peer}, device_id_type=MESH,
        )

    for peer in peers:
        res_copy(peer, me).start()
    inbox[me] = res_ref[me]
    rows = res_ref.shape[1]
    chunk = x_ref.shape[1] // n
    turned = res_ref[...].reshape(n * rows, 4 * DH).T
    for peer in range(n):
        term = jnp.dot(
            turned, x_ref[:, peer * chunk : (peer + 1) * chunk], preferred_element_type=jnp.float32
        ).astype(jnp.bfloat16)
        terms_out[peer, :DH] = term[:DH]
        terms_out[peer, DH:] = term[2 * DH :]
    for peer in peers:
        term_copy(peer, me).start()
    terms_in[me] = terms_out[me]
    for peer in peers:
        res_copy(peer, peer).wait_recv()

    def piece(which):
        return jnp.concatenate(
            [inbox[h, :, which * DH : (which + 1) * DH] for h in range(n)], axis=1
        )

    nt = (((1,), (1,)), ((), ()))
    grads = [piece(0), piece(2), piece(3)]
    weights = [wq_ref, wk_ref, wv_ref]
    for r in range(n_row):
        span = slice(r * cols, (r + 1) * cols)
        part = jnp.zeros((rows, cols), jnp.float32)
        for grad, weight in zip(grads, weights):
            part = part + lax.dot_general(
                grad, weight[span, :], nt, preferred_element_type=jnp.float32
            )
        part_out[r] = part.astype(jnp.bfloat16)
    for peer in row_peers:
        row_copy(peer, my_row).start()
    att_ref[...] = piece(1)
    for peer in peers:
        term_copy(peer, peer).wait_recv()
    for which, ref in enumerate((qg_ref, kg_ref, vg_ref)):
        for h in range(0, n, 2):
            pair = jnp.concatenate(
                [
                    terms_in[h, which * DH : (which + 1) * DH],
                    terms_in[h + 1, which * DH : (which + 1) * DH],
                ],
                axis=0,
            )
            ref[:, h * DH : (h + 2) * DH] = pair.astype(jnp.float32).T
    total = part_out[my_row].astype(jnp.float32)
    for peer in row_peers:
        row_copy(peer, peer).wait_recv()
        total = total + part_in[peer].astype(jnp.float32)
    node_ref[...] = total
    for peer in peers:
        res_copy(peer, me).wait_send()
        term_copy(peer, me).wait_send()
    for peer in row_peers:
        row_copy(peer, my_row).wait_send()


def collect_grads(res, x_all, query_weight, key_weight, value_weight, n, n_row):
    rows = res.shape[1]
    depth = x_all.shape[1]
    cols = depth // n_row
    chunk = depth // n
    head_cols = n * DH
    vmem = pl.BlockSpec(memory_space=pltpu.VMEM)
    dma = pltpu.SemaphoreType.DMA
    return pl.pallas_call(
        functools.partial(collect_kernel, n, n_row),
        out_shape=(
            jax.ShapeDtypeStruct((rows, head_cols), jnp.bfloat16),
            jax.ShapeDtypeStruct((rows, cols), jnp.float32),
            jax.ShapeDtypeStruct((chunk, head_cols), jnp.float32),
            jax.ShapeDtypeStruct((chunk, head_cols), jnp.float32),
            jax.ShapeDtypeStruct((chunk, head_cols), jnp.float32),
        ),
        in_specs=[vmem] * 5,
        out_specs=(vmem,) * 5,
        scratch_shapes=[
            pltpu.VMEM(res.shape, jnp.bfloat16),
            pltpu.VMEM((n, 3 * DH, chunk), jnp.bfloat16),
            pltpu.VMEM((n, 3 * DH, chunk), jnp.bfloat16),
            pltpu.VMEM((n_row, rows, cols), jnp.bfloat16),
            pltpu.VMEM((n_row, rows, cols), jnp.bfloat16),
            dma((n,)), dma((n,)), dma((n,)), dma((n,)), dma((n_row,)), dma((n_row,)),
        ],
        compiler_params=pltpu.CompilerParams(
            collective_id=1, has_side_effects=True, vmem_limit_bytes=40 << 20
        ),
        name="collect_grads",
    )(res, x_all, query_weight, key_weight, value_weight)


def per_device_heads(
    n, n_row, node_states, query_weight, key_weight, value_weight, output_grad, pair_list, pair_count
):
    blocks = node_states.shape[0] // BLK
    slots = pair_list.shape[1]
    listed = jnp.pad(pair_list[0].T, ((0, 0), (0, BLK - slots)))
    total = jnp.broadcast_to(pair_count[0], (6, BLK))
    codes = jnp.concatenate([listed, total], axis=0)
    x_all = lax.all_gather(node_states, "col", axis=0, tiled=True)
    heads, codes_all = spread(
        node_states, query_weight, key_weight, value_weight, output_grad, codes, n
    )
    res = attend(heads, codes_all, n, blocks)
    return collect_grads(res, x_all, query_weight, key_weight, value_weight, n, n_row)


def per_device(mesh, *arrays):
    n, n_row = mesh.shape["col"], mesh.shape["row"]
    node_states, query_weight, pair_list = arrays[0], arrays[1], arrays[5]
    blocks = node_states.shape[0] // BLK
    one_head_each = query_weight.shape[1] == n * DH and n % 2 == 0
    tiled = (n * blocks) % GROUP == 0 and pair_list.shape[1] <= BLK
    lanes = node_states.shape[1] % (n * BLK) == 0 and node_states.shape[1] % (n_row * BLK) == 0
    if one_head_each and tiled and lanes:
        return per_device_heads(n, n_row, *arrays)
    return per_device_slots(*arrays)


def solution(mesh):
    return jax.shard_map(
        functools.partial(per_device, mesh),
        mesh=mesh,
        in_specs=(
            P(("groups", "col"), None),
            P(None, "row"),
            P(None, "row"),
            P(None, "row"),
            P(("groups", "col"), "row"),
            P(("groups", "col"), None, None),
            P(("groups", "col")),
        ),
        out_specs=(
            P(("groups", "col"), "row"),
            P(("groups", "col"), "row"),
            P(("groups", "col"), "row"),
            P(("groups", "col"), "row"),
            P(("groups", "col"), "row"),
        ),
        check_vma=False,
    )
```

```python
import functools
import math

import jax
import jax.numpy as jnp
from jax import lax
from jax.experimental import pallas as pl
from jax.experimental.pallas import tpu as pltpu
from jax.sharding import PartitionSpec as P

DH = 64
BLK = 128


LOWEST = -1e30
EXACT = lax.Precision.HIGHEST


def slot_batch(pair_rows, pair_total, turn_index, width, blocks):
    start = turn_index * width
    query_block = pair_rows[:, 0]
    key_block = pair_rows[:, 1]
    slot_live = start + jnp.arange(width, dtype=jnp.int32) < pair_total
    owners = jnp.logical_and(
        query_block[:, None] == jnp.arange(blocks, dtype=jnp.int32)[None, :], slot_live[:, None]
    )
    return (query_block, key_block, slot_live, owners)


def batch_tiles(query_tiles, table_tiles, query_block, key_block, head_cols, factor):
    head_count = head_cols // DH
    width = query_block.shape[0]
    query_pick = jnp.take(query_tiles, query_block, axis=0)
    table_pick = jnp.take(table_tiles, key_block, axis=0)
    key_pick = table_pick[:, :, :head_cols].reshape(width, BLK, head_count, DH)
    value_pick = table_pick[:, :, head_cols:].reshape(width, BLK, head_count, DH)
    scores = (
        jnp.einsum("sihd,sjhd->shij", query_pick, key_pick, preferred_element_type=jnp.float32)
        * factor
    )
    return (query_pick, key_pick, value_pick, scores)


def batch_weights(scores, row_top, totals, query_block, slot_live):
    top_pick = jnp.take(row_top, query_block, axis=0)
    total_pick = jnp.take(totals, query_block, axis=0)
    weights = jnp.exp(scores - top_pick[..., None]) / total_pick[..., None]
    return jnp.where(slot_live[:, None, None, None], weights, 0.0).astype(jnp.bfloat16)


def per_device_slots(
    node_states, query_weight, key_weight, value_weight, output_grad, pair_list, pair_count
):
    head_cols = query_weight.shape[1]
    head_count = head_cols // DH
    panel_rows = node_states.shape[0]
    blocks = panel_rows // BLK
    factor = 1.0 / math.sqrt(DH)
    pair_rows = pair_list[0]
    pair_total = pair_count[0]
    width = math.gcd(pair_rows.shape[0], 32)
    turns = (pair_total + width - 1) // width
    queries = jnp.dot(node_states, query_weight, preferred_element_type=jnp.float32).astype(
        jnp.bfloat16
    )
    keys_here = jnp.dot(node_states, key_weight, preferred_element_type=jnp.float32).astype(
        jnp.bfloat16
    )
    values_here = jnp.dot(node_states, value_weight, preferred_element_type=jnp.float32).astype(
        jnp.bfloat16
    )
    local_table = jnp.concatenate([keys_here, values_here], axis=1)
    key_table = lax.all_gather(local_table, "col", axis=0, tiled=True)
    key_blocks_all = key_table.shape[0] // BLK
    query_tiles = queries.reshape(blocks, BLK, head_count, DH)
    table_tiles = key_table.reshape(key_blocks_all, BLK, 2 * head_cols)

    def stats_turn(turn_index, state_pair):
        row_top, totals = state_pair
        query_block, key_block, slot_live, owners = slot_batch(
            pair_rows, pair_total, turn_index, width, blocks
        )
        scores = batch_tiles(query_tiles, table_tiles, query_block, key_block, head_cols, factor)[3]
        pair_top = jnp.max(scores, axis=3)
        block_top = jnp.max(jnp.where(owners[:, :, None, None], pair_top[:, None], LOWEST), axis=0)
        new_top = jnp.maximum(row_top, block_top)
        top_pick = jnp.take(new_top, query_block, axis=0)
        exp_terms = jnp.where(
            slot_live[:, None, None, None], jnp.exp(scores - top_pick[..., None]), 0.0
        )
        added = jnp.einsum(
            "sn,shi->nhi", owners.astype(jnp.float32), jnp.sum(exp_terms, axis=3), precision=EXACT
        )
        totals = totals * jnp.exp(row_top - new_top) + added
        return (new_top, totals)

    start_top = jnp.full((blocks, head_count, BLK), LOWEST, jnp.float32)
    start_total = jnp.zeros((blocks, head_count, BLK), jnp.float32)
    row_top, totals = lax.fori_loop(0, turns, stats_turn, (start_top, start_total))

    def attend_turn(turn_index, output):
        query_block, key_block, slot_live, owners = slot_batch(
            pair_rows, pair_total, turn_index, width, blocks
        )
        query_pick, key_pick, value_pick, scores = batch_tiles(
            query_tiles, table_tiles, query_block, key_block, head_cols, factor
        )
        weights = batch_weights(scores, row_top, totals, query_block, slot_live)
        update = jnp.einsum(
            "shij,sjhd->sihd", weights, value_pick, preferred_element_type=jnp.float32
        )
        return output + jnp.einsum(
            "sn,sihd->nihd", owners.astype(jnp.float32), update, precision=EXACT
        )

    output = lax.fori_loop(
        0, turns, attend_turn, jnp.zeros((blocks, BLK, head_count, DH), jnp.float32)
    )
    attended = output.reshape(panel_rows, head_cols).astype(jnp.bfloat16)
    grad_tiles = output_grad.reshape(blocks, BLK, head_count, DH)
    deltas = jnp.sum(grad_tiles.astype(jnp.float32) * output, axis=3)
    back_table = lax.all_gather(local_table, "col", axis=0, tiled=True)
    back_tiles = back_table.reshape(key_blocks_all, BLK, 2 * head_cols)

    def backward_turn(turn_index, state_pair):
        grad_rows, key_grads = state_pair
        query_block, key_block, slot_live, owners = slot_batch(
            pair_rows, pair_total, turn_index, width, blocks
        )
        query_pick, key_pick, value_pick, scores = batch_tiles(
            query_tiles, back_tiles, query_block, key_block, head_cols, factor
        )
        weights = batch_weights(scores, row_top, totals, query_block, slot_live)
        grad_pick = jnp.take(grad_tiles, query_block, axis=0)
        value_part = jnp.einsum(
            "shij,sihd->sjhd", weights, grad_pick, preferred_element_type=jnp.float32
        )
        prob_grad = jnp.einsum(
            "sihd,sjhd->shij", grad_pick, value_pick, preferred_element_type=jnp.float32
        )
        delta_pick = jnp.transpose(jnp.take(deltas, query_block, axis=0), (0, 2, 1))
        score_grad = (weights.astype(jnp.float32) * (prob_grad - delta_pick[..., None])).astype(
            jnp.bfloat16
        )
        query_part = (
            jnp.einsum("shij,sjhd->sihd", score_grad, key_pick, preferred_element_type=jnp.float32)
            * factor
        )
        key_part = (
            jnp.einsum(
                "shij,sihd->sjhd", score_grad, query_pick, preferred_element_type=jnp.float32
            )
            * factor
        )
        grad_rows = grad_rows + jnp.einsum(
            "sn,sihd->nihd", owners.astype(jnp.float32), query_part, precision=EXACT
        )
        rows_update = jnp.concatenate(
            [key_part.reshape(width, BLK, head_cols), value_part.reshape(width, BLK, head_cols)],
            axis=2,
        )
        key_grads = key_grads + jax.ops.segment_sum(
            rows_update, key_block, num_segments=key_blocks_all
        )
        return (grad_rows, key_grads)

    start_rows = jnp.zeros((blocks, BLK, head_count, DH), jnp.float32)
    start_keys = jnp.zeros((key_blocks_all, BLK, 2 * head_cols), jnp.float32)
    grad_rows, key_grads = lax.fori_loop(0, turns, backward_turn, (start_rows, start_keys))
    key_grads = key_grads.reshape(key_blocks_all * BLK, 2 * head_cols)
    pair_grads = lax.psum_scatter(
        key_grads.astype(jnp.bfloat16), "col", scatter_dimension=0, tiled=True
    ).astype(jnp.float32)
    query_rows_grad = grad_rows.reshape(panel_rows, head_cols).astype(jnp.bfloat16)
    key_rows_grad = pair_grads[:, :head_cols].astype(jnp.bfloat16)
    value_rows_grad = pair_grads[:, head_cols:].astype(jnp.bfloat16)
    contract = (((1,), (1,)), ((), ()))
    partial_sum = lax.dot_general(
        query_rows_grad, query_weight, contract, preferred_element_type=jnp.float32
    )
    partial_sum = partial_sum + lax.dot_general(
        key_rows_grad, key_weight, contract, preferred_element_type=jnp.float32
    )
    partial_sum = partial_sum + lax.dot_general(
        value_rows_grad, value_weight, contract, preferred_element_type=jnp.float32
    )
    node_grad = lax.psum_scatter(
        partial_sum.astype(jnp.bfloat16), "row", scatter_dimension=1, tiled=True
    ).astype(jnp.float32)
    over_nodes = (((0,), (0,)), ((), ()))
    query_term = lax.dot_general(
        node_states, query_rows_grad, over_nodes, preferred_element_type=jnp.float32
    )
    key_term = lax.dot_general(
        node_states, key_rows_grad, over_nodes, preferred_element_type=jnp.float32
    )
    value_term = lax.dot_general(
        node_states, value_rows_grad, over_nodes, preferred_element_type=jnp.float32
    )
    query_grad, key_grad, value_grad = (
        lax.psum_scatter(
            query_term.astype(jnp.bfloat16), "col", scatter_dimension=0, tiled=True
        ).astype(jnp.float32),
        lax.psum_scatter(
            key_term.astype(jnp.bfloat16), "col", scatter_dimension=0, tiled=True
        ).astype(jnp.float32),
        lax.psum_scatter(
            value_term.astype(jnp.bfloat16), "col", scatter_dimension=0, tiled=True
        ).astype(jnp.float32),
    )
    return (attended, node_grad, query_grad, key_grad, value_grad)


MESH = pl.DeviceIdType.MESH
GROUP = 4


def meet(axes):
    barrier = pltpu.get_barrier_semaphore()
    total = 0
    for axis, count in axes:
        me = lax.axis_index(axis)
        for step in range(1, count):
            peer = lax.rem(me + step, count)
            pl.semaphore_signal(barrier, inc=1, device_id={axis: peer}, device_id_type=MESH)
            total += 1
    pl.semaphore_wait(barrier, total)


def spread_kernel(
    n, x_ref, wq_ref, wk_ref, wv_ref, grad_ref, code_ref, heads_ref, codes_ref, x_all,
    grads, weights, outbox, inbox, own_sem, load_sem, grad_send, grad_recv, code_send, code_recv,
    chain_send, chain_recv, core_send, core_recv, row_send, row_recv,
):
    me = lax.axis_index("col")
    half = lax.axis_index("row")
    other = 1 - half
    near = n // 2
    z = lax.div(me, 2)
    k = lax.rem(me, 2)
    twin = 2 * z + 1 - k

    loads = [
        pltpu.make_async_copy(
            ref.at[:, pl.ds(pl.multiple_of(z * 2 * DH, 2 * DH), 2 * DH)],
            weights.at[i],
            load_sem.at[i],
        )
        for i, ref in enumerate((wq_ref, wk_ref, wv_ref))
    ]
    loads.append(pltpu.make_async_copy(grad_ref, grads, load_sem.at[3]))
    loads.append(pltpu.make_async_copy(x_ref, x_all.at[me], load_sem.at[4]))
    loads.append(pltpu.make_async_copy(code_ref, codes_ref.at[me], load_sem.at[5]))
    for load in loads:
        load.start()
    meet([("col", n), ("row", 2)])

    def code_copy(peer, slot):
        return pltpu.make_async_remote_copy(
            src_ref=code_ref, dst_ref=codes_ref.at[slot], send_sem=code_send.at[peer],
            recv_sem=code_recv.at[slot], device_id={"col": peer}, device_id_type=MESH,
        )

    def grad_copy(peer, slot):
        return pltpu.make_async_remote_copy(
            src_ref=outbox.at[peer], dst_ref=inbox.at[slot], send_sem=grad_send.at[peer],
            recv_sem=grad_recv.at[slot], device_id={"col": peer}, device_id_type=MESH,
        )

    def chain_copy(src, origin, side, target):
        return pltpu.make_async_remote_copy(
            src_ref=src, dst_ref=x_all.at[2 * origin + k, half],
            send_sem=chain_send.at[side, origin], recv_sem=chain_recv.at[origin],
            device_id={"col": 2 * target + k}, device_id_type=MESH,
        )

    def core_copy(src, origin, part, core):
        return pltpu.make_async_remote_copy(
            src_ref=src, dst_ref=x_all.at[2 * origin + core, part],
            send_sem=core_send.at[origin, part], recv_sem=core_recv.at[origin, part],
            device_id={"col": twin}, device_id_type=MESH,
        )

    def row_copy(src, origin, part):
        return pltpu.make_async_remote_copy(
            src_ref=src, dst_ref=x_all.at[2 * origin + k, part],
            send_sem=row_send.at[origin], recv_sem=row_recv.at[origin],
            device_id={"row": other}, device_id_type=MESH,
        )

    peers = [lax.rem(me + step, n) for step in range(1, n)]
    up, down = z + 1 < near, z >= 1

    @pl.when(up)
    def _():
        chain_copy(x_ref.at[half], z, 0, z + 1).start()

    @pl.when(down)
    def _():
        chain_copy(x_ref.at[half], z, 1, z - 1).start()

    for part in range(2):
        core_copy(x_ref.at[part], z, part, k).start()
    for peer in peers:
        code_copy(peer, me).start()
    loads[3].wait()
    deep = grads.shape[0] // 2
    for head in range(n):
        cols = slice(head * DH, (head + 1) * DH)
        outbox[head] = jnp.concatenate([grads[:deep, cols], grads[deep:, cols]], axis=1)
    for peer in peers:
        grad_copy(peer, me).start()
    own = pltpu.make_async_copy(outbox.at[me], inbox.at[me], own_sem)
    own.start()

    sides = []
    for d in range(1, near):
        sides.append((z - d, z - d >= 0, up, 0, z + 1))
        sides.append((z + d, z + d < near, down, 1, z - 1))

    def through_row(origin, there):
        @pl.when(there)
        def _():
            block = x_all.at[2 * origin + k, other]
            row_copy(block, origin, other).wait_recv()
            core_copy(block, origin, other, k).start()

    for step, (origin, there, onward, side, target) in enumerate(sides):
        @pl.when(there)
        def _(origin=origin, onward=onward, side=side, target=target):
            block = x_all.at[2 * origin + k, half]
            chain_copy(block, origin, side, z).wait_recv()

            @pl.when(onward)
            def _():
                chain_copy(block, origin, side, target).start()

            row_copy(block, origin, half).start()
            core_copy(block, origin, half, k).start()

        if step >= 2:
            through_row(*sides[step - 2][:2])
    for origin, there, _, _, _ in sides[-2:]:
        through_row(origin, there)
    for load in loads[:3] + loads[4:]:
        load.wait()
    factor = 1.0 / math.sqrt(DH)
    picked = [
        jnp.where(k == 0, weights[i, :, :DH], weights[i, :, DH:]) for i in range(3)
    ]
    weight = jnp.concatenate([picked[0], picked[0], picked[1], picked[2]], axis=1)
    own.wait()
    for origin in range(near):
        for part in range(2):
            core_copy(x_all.at[2 * origin + 1 - k, part], origin, part, 1 - k).wait_recv()
    for peer in peers:
        code_copy(peer, peer).wait_recv()
        grad_copy(peer, peer).wait_recv()
    for panel in range(n):
        x = x_all[panel].reshape(2 * deep, x_all.shape[3])
        made = jnp.dot(x, weight, preferred_element_type=jnp.float32).astype(jnp.bfloat16)
        queries = (made[:, :DH].astype(jnp.float32) * factor).astype(jnp.bfloat16)
        box = inbox[panel]
        heads_ref[panel, :deep, : 2 * DH] = jnp.concatenate([queries[:deep], box[:, :DH]], axis=1)
        heads_ref[panel, deep:, : 2 * DH] = jnp.concatenate([queries[deep:], box[:, DH:]], axis=1)
        heads_ref[panel, :, 2 * DH :] = made[:, 2 * DH :]
    for peer in peers:
        code_copy(peer, me).wait_send()
        grad_copy(peer, me).wait_send()

    @pl.when(up)
    def _():
        chain_copy(x_ref.at[half], z, 0, z + 1).wait_send()

    @pl.when(down)
    def _():
        chain_copy(x_ref.at[half], z, 1, z - 1).wait_send()

    for part in range(2):
        core_copy(x_ref.at[part], z, part, k).wait_send()
    for origin, there, onward, side, target in sides:
        @pl.when(there)
        def _(origin=origin, onward=onward, side=side, target=target):
            block = x_all.at[2 * origin + k, half]

            @pl.when(onward)
            def _():
                chain_copy(block, origin, side, target).wait_send()

            row_copy(block, origin, half).wait_send()
            core_copy(block, origin, half, k).wait_send()
            core_copy(x_all.at[2 * origin + k, other], origin, other, k).wait_send()


def spread(node_states, query_weight, key_weight, value_weight, output_grad, codes, n):
    rows, depth = node_states.shape
    width = 4 * DH
    near = n // 2
    vmem = pl.BlockSpec(memory_space=pltpu.VMEM)
    hbm = pl.BlockSpec(memory_space=pltpu.HBM)
    dma = pltpu.SemaphoreType.DMA
    return pl.pallas_call(
        functools.partial(spread_kernel, n),
        out_shape=(
            jax.ShapeDtypeStruct((n, rows, width), jnp.bfloat16),
            jax.ShapeDtypeStruct((n,) + codes.shape, jnp.int32),
            jax.ShapeDtypeStruct((n, 2, rows // 2, depth), jnp.bfloat16),
        ),
        in_specs=[hbm] * 5 + [vmem],
        out_specs=(vmem, vmem, vmem),
        scratch_shapes=[
            pltpu.VMEM(output_grad.shape, jnp.bfloat16),
            pltpu.VMEM((3, depth, 2 * DH), jnp.bfloat16),
            pltpu.VMEM((n, rows // 2, 2 * DH), jnp.bfloat16),
            pltpu.VMEM((n, rows // 2, 2 * DH), jnp.bfloat16),
            dma, dma((6,)), dma((n,)), dma((n,)), dma((n,)), dma((n,)),
            dma((2, near)), dma((near,)), dma((near, 2)), dma((near, 2)), dma((near,)), dma((near,)),
        ],
        compiler_params=pltpu.CompilerParams(
            collective_id=0, has_side_effects=True, vmem_limit_bytes=16 << 20
        ),
        cost_estimate=pl.CostEstimate(
            flops=6 * rows * depth * n * DH, bytes_accessed=40 << 20, transcendentals=0
        ),
        name="spread_heads",
    )(
        node_states.reshape(2, rows // 2, depth), query_weight, key_weight, value_weight,
        output_grad, codes,
    )


def attend_kernel(
    n, blocks, codes_ref, heads_ref, out_ref, pairs_acc, scores_buf, grads_buf, found, counts
):
    lanes = lax.broadcasted_iota(jnp.int32, (BLK, 2 * DH), 1)
    first = lanes < DH
    key_total = n * blocks
    nt = (((1,), (1,)), ((), ()))
    pairs_acc[...] = jnp.zeros_like(pairs_acc)

    def collect(panel):
        for q in range(blocks):
            counts[q] = 0
            for k in range(key_total):
                found[q, k] = 0
        total = codes_ref[panel, 2, 0]

        def one(slot, carry):
            q = codes_ref[panel, 0, slot]
            place = counts[q]
            found[q, place] = codes_ref[panel, 1, slot]
            counts[q] = place + 1
            return carry

        lax.fori_loop(0, total, one, 0)

    def work(panel, groups):
        width = GROUP * BLK
        stacks = []
        for q in range(blocks):
            both = heads_ref[panel, q * BLK : (q + 1) * BLK, : 2 * DH]
            zero = jnp.zeros_like(both)
            stacks.append(
                jnp.concatenate([jnp.where(first, both, zero), jnp.where(first, zero, both)], axis=0)
            )

        def table(q, g):
            parts = []
            for j in range(GROUP):
                k = found[q, g * GROUP + j]
                start = pl.multiple_of(lax.rem(k, blocks) * BLK, BLK)
                parts.append(heads_ref[lax.div(k, blocks), pl.ds(start, BLK), 2 * DH :])
            return jnp.concatenate(parts, axis=0)

        tops, totals, outs, deltas = [], [], [], []
        for q in range(blocks):
            top = jnp.full((BLK, BLK), LOWEST, jnp.float32)
            for g in range(groups):
                both = lax.dot_general(stacks[q], table(q, g), nt, preferred_element_type=jnp.float32)
                grads_buf[q, g] = both[BLK:]
                for j in range(GROUP):
                    tile = both[:BLK, j * BLK : (j + 1) * BLK]
                    live = g * GROUP + j < counts[q]
                    tile = jnp.where(live, tile, LOWEST)
                    scores_buf[q, g, :, j * BLK : (j + 1) * BLK] = tile
                    top = jnp.maximum(top, tile)
            tops.append(jnp.max(top, axis=1, keepdims=True))
        for q in range(blocks):
            total = jnp.zeros((BLK, BLK), jnp.float32)
            for g in range(groups):
                terms = jnp.exp(scores_buf[q, g] - tops[q])
                scores_buf[q, g] = terms
                for j in range(GROUP):
                    total = total + terms[:, j * BLK : (j + 1) * BLK]
            totals.append(1.0 / jnp.sum(total, axis=1, keepdims=True))
        for q in range(blocks):
            out = jnp.zeros((BLK, 2 * DH), jnp.float32)
            for g in range(groups):
                weights = (scores_buf[q, g] * totals[q]).astype(jnp.bfloat16)
                out = out + jnp.dot(weights, table(q, g), preferred_element_type=jnp.float32)
            outs.append(out)
            grad = stacks[q][BLK:].astype(jnp.float32)
            deltas.append(jnp.sum(grad * out, axis=1, keepdims=True))
        for q in range(blocks):
            rows_grad = jnp.zeros((BLK, 2 * DH), jnp.float32)
            turned = stacks[q].T
            for g in range(groups):
                weights = (scores_buf[q, g] * totals[q]).astype(jnp.bfloat16)
                score_grad = (
                    weights.astype(jnp.float32) * (grads_buf[q, g] - deltas[q])
                ).astype(jnp.bfloat16)
                rows_grad = rows_grad + jnp.dot(
                    score_grad, table(q, g), preferred_element_type=jnp.float32
                )
                pair = jnp.dot(
                    turned,
                    jnp.concatenate([score_grad, weights], axis=0),
                    preferred_element_type=jnp.float32,
                )
                for j in range(GROUP):
                    k = found[q, g * GROUP + j]
                    pairs_acc[k] = pairs_acc[k] + pair[:, j * BLK : (j + 1) * BLK]
            factor = 1.0 / math.sqrt(DH)
            out_ref[panel, q * BLK : (q + 1) * BLK, : 2 * DH] = jnp.where(
                first, rows_grad * factor, outs[q]
            ).astype(jnp.bfloat16)

    def one_panel(panel, carry):
        collect(panel)
        most = counts[0]
        for q in range(1, blocks):
            most = jnp.maximum(most, counts[q])
        groups = lax.div(most + (GROUP - 1), GROUP)
        for size in range(1, key_total // GROUP + 1):
            pl.when(groups == size)(functools.partial(work, panel, size))
        return carry

    lax.fori_loop(0, n, one_panel, 0)
    for k in range(key_total):
        row = (k % blocks) * BLK
        out_ref[k // blocks, row : row + BLK, 2 * DH :] = pairs_acc[k].T.astype(jnp.bfloat16)


def attend(heads, codes, n, blocks):
    key_total = n * blocks
    groups = key_total // GROUP
    tiles = key_total * key_total
    return pl.pallas_call(
        functools.partial(attend_kernel, n, blocks),
        out_shape=jax.ShapeDtypeStruct(heads.shape, jnp.bfloat16),
        in_specs=[
            pl.BlockSpec(memory_space=pltpu.SMEM),
            pl.BlockSpec(memory_space=pltpu.VMEM),
        ],
        out_specs=pl.BlockSpec(memory_space=pltpu.VMEM),
        scratch_shapes=[
            pltpu.VMEM((key_total, 2 * DH, BLK), jnp.float32),
            pltpu.VMEM((blocks, groups, BLK, GROUP * BLK), jnp.float32),
            pltpu.VMEM((blocks, groups, BLK, GROUP * BLK), jnp.float32),
            pltpu.SMEM((blocks, key_total), jnp.int32),
            pltpu.SMEM((blocks,), jnp.int32),
        ],
        compiler_params=pltpu.CompilerParams(vmem_limit_bytes=16 << 20),
        cost_estimate=pl.CostEstimate(
            flops=tiles * 24 * BLK * BLK * DH, bytes_accessed=80 << 20,
            transcendentals=tiles * BLK * BLK,
        ),
        name="attend_heads",
    )(codes, heads)


def collect_kernel(
    n, n_row, res_ref, x_ref, wq_ref, wk_ref, wv_ref,
    att_ref, node_ref, qg_ref, kg_ref, vg_ref,
    inbox, terms_out, terms_in, part_out, part_in,
    send_sem, recv_sem, term_send, term_recv, row_send, row_recv,
):
    me = lax.axis_index("col")
    my_row = lax.axis_index("row")
    meet([("col", n), ("row", n_row)])
    peers = [lax.rem(me + step, n) for step in range(1, n)]
    row_peers = [lax.rem(my_row + step, n_row) for step in range(1, n_row)]
    cols = part_out.shape[2]

    def res_copy(peer, slot):
        return pltpu.make_async_remote_copy(
            src_ref=res_ref.at[peer], dst_ref=inbox.at[slot], send_sem=send_sem.at[peer],
            recv_sem=recv_sem.at[slot], device_id={"col": peer}, device_id_type=MESH,
        )

    def term_copy(peer, slot):
        return pltpu.make_async_remote_copy(
            src_ref=terms_out.at[peer], dst_ref=terms_in.at[slot], send_sem=term_send.at[peer],
            recv_sem=term_recv.at[slot], device_id={"col": peer}, device_id_type=MESH,
        )

    def row_copy(peer, slot):
        return pltpu.make_async_remote_copy(
            src_ref=part_out.at[peer], dst_ref=part_in.at[slot], send_sem=row_send.at[peer],
            recv_sem=row_recv.at[slot], device_id={"row": peer}, device_id_type=MESH,
        )

    for peer in peers:
        res_copy(peer, me).start()
    inbox[me] = res_ref[me]
    rows = res_ref.shape[1]
    depth = x_ref.shape[3]
    chunk = depth // n
    turned = res_ref[...].reshape(n * rows, 4 * DH).T
    for peer in range(n):
        term = jnp.dot(
            turned,
            x_ref[:, :, :, peer * chunk : (peer + 1) * chunk].reshape(n * rows, chunk),
            preferred_element_type=jnp.float32,
        ).astype(jnp.bfloat16)
        terms_out[peer, :DH] = term[:DH]
        terms_out[peer, DH:] = term[2 * DH :]
    terms_in[me] = terms_out[me]
    for peer in peers:
        res_copy(peer, peer).wait_recv()
    for peer in peers:
        term_copy(peer, me).start()

    def piece(which):
        return jnp.concatenate(
            [inbox[h, :, which * DH : (which + 1) * DH] for h in range(n)], axis=1
        )

    nt = (((1,), (1,)), ((), ()))
    grads = [piece(0), piece(2), piece(3)]
    weights = [wq_ref, wk_ref, wv_ref]
    for r in range(n_row):
        span = slice(r * cols, (r + 1) * cols)
        part = jnp.zeros((rows, cols), jnp.float32)
        for grad, weight in zip(grads, weights):
            part = part + lax.dot_general(
                grad, weight[span, :], nt, preferred_element_type=jnp.float32
            )
        part_out[r] = part.astype(jnp.bfloat16)
    for peer in row_peers:
        row_copy(peer, my_row).start()
    att_ref[...] = piece(1)
    for peer in peers:
        term_copy(peer, peer).wait_recv()
    for which, ref in enumerate((qg_ref, kg_ref, vg_ref)):
        for h in range(0, n, 2):
            pair = jnp.concatenate(
                [
                    terms_in[h, which * DH : (which + 1) * DH],
                    terms_in[h + 1, which * DH : (which + 1) * DH],
                ],
                axis=0,
            )
            ref[:, h * DH : (h + 2) * DH] = pair.astype(jnp.float32).T
    total = part_out[my_row].astype(jnp.float32)
    for peer in row_peers:
        row_copy(peer, peer).wait_recv()
        total = total + part_in[peer].astype(jnp.float32)
    node_ref[...] = total
    for peer in peers:
        res_copy(peer, me).wait_send()
        term_copy(peer, me).wait_send()
    for peer in row_peers:
        row_copy(peer, my_row).wait_send()


def collect_grads(res, x_all, query_weight, key_weight, value_weight, n, n_row):
    rows = res.shape[1]
    depth = x_all.shape[3]
    cols = depth // n_row
    chunk = depth // n
    head_cols = n * DH
    vmem = pl.BlockSpec(memory_space=pltpu.VMEM)
    dma = pltpu.SemaphoreType.DMA
    return pl.pallas_call(
        functools.partial(collect_kernel, n, n_row),
        out_shape=(
            jax.ShapeDtypeStruct((rows, head_cols), jnp.bfloat16),
            jax.ShapeDtypeStruct((rows, cols), jnp.float32),
            jax.ShapeDtypeStruct((chunk, head_cols), jnp.float32),
            jax.ShapeDtypeStruct((chunk, head_cols), jnp.float32),
            jax.ShapeDtypeStruct((chunk, head_cols), jnp.float32),
        ),
        in_specs=[vmem] * 5,
        out_specs=(vmem,) * 5,
        scratch_shapes=[
            pltpu.VMEM(res.shape, jnp.bfloat16),
            pltpu.VMEM((n, 3 * DH, chunk), jnp.bfloat16),
            pltpu.VMEM((n, 3 * DH, chunk), jnp.bfloat16),
            pltpu.VMEM((n_row, rows, cols), jnp.bfloat16),
            pltpu.VMEM((n_row, rows, cols), jnp.bfloat16),
            dma((n,)), dma((n,)), dma((n,)), dma((n,)), dma((n_row,)), dma((n_row,)),
        ],
        compiler_params=pltpu.CompilerParams(
            collective_id=1, has_side_effects=True, vmem_limit_bytes=20 << 20
        ),
        name="collect_grads",
    )(res, x_all, query_weight, key_weight, value_weight)


def per_device_heads(
    n, n_row, node_states, query_weight, key_weight, value_weight, output_grad, pair_list, pair_count
):
    blocks = node_states.shape[0] // BLK
    slots = pair_list.shape[1]
    listed = jnp.pad(pair_list[0].T, ((0, 0), (0, BLK - slots)))
    total = jnp.broadcast_to(pair_count[0], (6, BLK))
    codes = jnp.concatenate([listed, total], axis=0)
    heads, codes_all, x_all = spread(
        node_states, query_weight, key_weight, value_weight, output_grad, codes, n
    )
    res = attend(heads, codes_all, n, blocks)
    return collect_grads(res, x_all, query_weight, key_weight, value_weight, n, n_row)


def per_device(mesh, *arrays):
    n, n_row = mesh.shape["col"], mesh.shape["row"]
    node_states, query_weight, pair_list = arrays[0], arrays[1], arrays[5]
    blocks = node_states.shape[0] // BLK
    one_head_each = query_weight.shape[1] == n * DH and n % 2 == 0 and n_row == 2
    tiled = (n * blocks) % GROUP == 0 and pair_list.shape[1] <= BLK
    lanes = node_states.shape[1] % (n * BLK) == 0 and node_states.shape[1] % (n_row * BLK) == 0
    if one_head_each and tiled and lanes:
        return per_device_heads(n, n_row, *arrays)
    return per_device_slots(*arrays)


def solution(mesh):
    return jax.shard_map(
        functools.partial(per_device, mesh),
        mesh=mesh,
        in_specs=(
            P(("groups", "col"), None),
            P(None, "row"),
            P(None, "row"),
            P(None, "row"),
            P(("groups", "col"), "row"),
            P(("groups", "col"), None, None),
            P(("groups", "col")),
        ),
        out_specs=(
            P(("groups", "col"), "row"),
            P(("groups", "col"), "row"),
            P(("groups", "col"), "row"),
            P(("groups", "col"), "row"),
            P(("groups", "col"), "row"),
        ),
        check_vma=False,
    )
```

```python
import functools
import math

import jax
import jax.numpy as jnp
from jax import lax
from jax.experimental import pallas as pl
from jax.experimental.pallas import tpu as pltpu
from jax.sharding import PartitionSpec as P

DH = 64
BLK = 128


LOWEST = -1e30
EXACT = lax.Precision.HIGHEST


def slot_batch(pair_rows, pair_total, turn_index, width, blocks):
    start = turn_index * width
    query_block = pair_rows[:, 0]
    key_block = pair_rows[:, 1]
    slot_live = start + jnp.arange(width, dtype=jnp.int32) < pair_total
    owners = jnp.logical_and(
        query_block[:, None] == jnp.arange(blocks, dtype=jnp.int32)[None, :], slot_live[:, None]
    )
    return (query_block, key_block, slot_live, owners)


def batch_tiles(query_tiles, table_tiles, query_block, key_block, head_cols, factor):
    head_count = head_cols // DH
    width = query_block.shape[0]
    query_pick = jnp.take(query_tiles, query_block, axis=0)
    table_pick = jnp.take(table_tiles, key_block, axis=0)
    key_pick = table_pick[:, :, :head_cols].reshape(width, BLK, head_count, DH)
    value_pick = table_pick[:, :, head_cols:].reshape(width, BLK, head_count, DH)
    scores = (
        jnp.einsum("sihd,sjhd->shij", query_pick, key_pick, preferred_element_type=jnp.float32)
        * factor
    )
    return (query_pick, key_pick, value_pick, scores)


def batch_weights(scores, row_top, totals, query_block, slot_live):
    top_pick = jnp.take(row_top, query_block, axis=0)
    total_pick = jnp.take(totals, query_block, axis=0)
    weights = jnp.exp(scores - top_pick[..., None]) / total_pick[..., None]
    return jnp.where(slot_live[:, None, None, None], weights, 0.0).astype(jnp.bfloat16)


def per_device_slots(
    node_states, query_weight, key_weight, value_weight, output_grad, pair_list, pair_count
):
    head_cols = query_weight.shape[1]
    head_count = head_cols // DH
    panel_rows = node_states.shape[0]
    blocks = panel_rows // BLK
    factor = 1.0 / math.sqrt(DH)
    pair_rows = pair_list[0]
    pair_total = pair_count[0]
    width = math.gcd(pair_rows.shape[0], 32)
    turns = (pair_total + width - 1) // width
    queries = jnp.dot(node_states, query_weight, preferred_element_type=jnp.float32).astype(
        jnp.bfloat16
    )
    keys_here = jnp.dot(node_states, key_weight, preferred_element_type=jnp.float32).astype(
        jnp.bfloat16
    )
    values_here = jnp.dot(node_states, value_weight, preferred_element_type=jnp.float32).astype(
        jnp.bfloat16
    )
    local_table = jnp.concatenate([keys_here, values_here], axis=1)
    key_table = lax.all_gather(local_table, "col", axis=0, tiled=True)
    key_blocks_all = key_table.shape[0] // BLK
    query_tiles = queries.reshape(blocks, BLK, head_count, DH)
    table_tiles = key_table.reshape(key_blocks_all, BLK, 2 * head_cols)

    def stats_turn(turn_index, state_pair):
        row_top, totals = state_pair
        query_block, key_block, slot_live, owners = slot_batch(
            pair_rows, pair_total, turn_index, width, blocks
        )
        scores = batch_tiles(query_tiles, table_tiles, query_block, key_block, head_cols, factor)[3]
        pair_top = jnp.max(scores, axis=3)
        block_top = jnp.max(jnp.where(owners[:, :, None, None], pair_top[:, None], LOWEST), axis=0)
        new_top = jnp.maximum(row_top, block_top)
        top_pick = jnp.take(new_top, query_block, axis=0)
        exp_terms = jnp.where(
            slot_live[:, None, None, None], jnp.exp(scores - top_pick[..., None]), 0.0
        )
        added = jnp.einsum(
            "sn,shi->nhi", owners.astype(jnp.float32), jnp.sum(exp_terms, axis=3), precision=EXACT
        )
        totals = totals * jnp.exp(row_top - new_top) + added
        return (new_top, totals)

    start_top = jnp.full((blocks, head_count, BLK), LOWEST, jnp.float32)
    start_total = jnp.zeros((blocks, head_count, BLK), jnp.float32)
    row_top, totals = lax.fori_loop(0, turns, stats_turn, (start_top, start_total))

    def attend_turn(turn_index, output):
        query_block, key_block, slot_live, owners = slot_batch(
            pair_rows, pair_total, turn_index, width, blocks
        )
        query_pick, key_pick, value_pick, scores = batch_tiles(
            query_tiles, table_tiles, query_block, key_block, head_cols, factor
        )
        weights = batch_weights(scores, row_top, totals, query_block, slot_live)
        update = jnp.einsum(
            "shij,sjhd->sihd", weights, value_pick, preferred_element_type=jnp.float32
        )
        return output + jnp.einsum(
            "sn,sihd->nihd", owners.astype(jnp.float32), update, precision=EXACT
        )

    output = lax.fori_loop(
        0, turns, attend_turn, jnp.zeros((blocks, BLK, head_count, DH), jnp.float32)
    )
    attended = output.reshape(panel_rows, head_cols).astype(jnp.bfloat16)
    grad_tiles = output_grad.reshape(blocks, BLK, head_count, DH)
    deltas = jnp.sum(grad_tiles.astype(jnp.float32) * output, axis=3)
    back_table = lax.all_gather(local_table, "col", axis=0, tiled=True)
    back_tiles = back_table.reshape(key_blocks_all, BLK, 2 * head_cols)

    def backward_turn(turn_index, state_pair):
        grad_rows, key_grads = state_pair
        query_block, key_block, slot_live, owners = slot_batch(
            pair_rows, pair_total, turn_index, width, blocks
        )
        query_pick, key_pick, value_pick, scores = batch_tiles(
            query_tiles, back_tiles, query_block, key_block, head_cols, factor
        )
        weights = batch_weights(scores, row_top, totals, query_block, slot_live)
        grad_pick = jnp.take(grad_tiles, query_block, axis=0)
        value_part = jnp.einsum(
            "shij,sihd->sjhd", weights, grad_pick, preferred_element_type=jnp.float32
        )
        prob_grad = jnp.einsum(
            "sihd,sjhd->shij", grad_pick, value_pick, preferred_element_type=jnp.float32
        )
        delta_pick = jnp.transpose(jnp.take(deltas, query_block, axis=0), (0, 2, 1))
        score_grad = (weights.astype(jnp.float32) * (prob_grad - delta_pick[..., None])).astype(
            jnp.bfloat16
        )
        query_part = (
            jnp.einsum("shij,sjhd->sihd", score_grad, key_pick, preferred_element_type=jnp.float32)
            * factor
        )
        key_part = (
            jnp.einsum(
                "shij,sihd->sjhd", score_grad, query_pick, preferred_element_type=jnp.float32
            )
            * factor
        )
        grad_rows = grad_rows + jnp.einsum(
            "sn,sihd->nihd", owners.astype(jnp.float32), query_part, precision=EXACT
        )
        rows_update = jnp.concatenate(
            [key_part.reshape(width, BLK, head_cols), value_part.reshape(width, BLK, head_cols)],
            axis=2,
        )
        key_grads = key_grads + jax.ops.segment_sum(
            rows_update, key_block, num_segments=key_blocks_all
        )
        return (grad_rows, key_grads)

    start_rows = jnp.zeros((blocks, BLK, head_count, DH), jnp.float32)
    start_keys = jnp.zeros((key_blocks_all, BLK, 2 * head_cols), jnp.float32)
    grad_rows, key_grads = lax.fori_loop(0, turns, backward_turn, (start_rows, start_keys))
    key_grads = key_grads.reshape(key_blocks_all * BLK, 2 * head_cols)
    pair_grads = lax.psum_scatter(
        key_grads.astype(jnp.bfloat16), "col", scatter_dimension=0, tiled=True
    ).astype(jnp.float32)
    query_rows_grad = grad_rows.reshape(panel_rows, head_cols).astype(jnp.bfloat16)
    key_rows_grad = pair_grads[:, :head_cols].astype(jnp.bfloat16)
    value_rows_grad = pair_grads[:, head_cols:].astype(jnp.bfloat16)
    contract = (((1,), (1,)), ((), ()))
    partial_sum = lax.dot_general(
        query_rows_grad, query_weight, contract, preferred_element_type=jnp.float32
    )
    partial_sum = partial_sum + lax.dot_general(
        key_rows_grad, key_weight, contract, preferred_element_type=jnp.float32
    )
    partial_sum = partial_sum + lax.dot_general(
        value_rows_grad, value_weight, contract, preferred_element_type=jnp.float32
    )
    node_grad = lax.psum_scatter(
        partial_sum.astype(jnp.bfloat16), "row", scatter_dimension=1, tiled=True
    ).astype(jnp.float32)
    over_nodes = (((0,), (0,)), ((), ()))
    query_term = lax.dot_general(
        node_states, query_rows_grad, over_nodes, preferred_element_type=jnp.float32
    )
    key_term = lax.dot_general(
        node_states, key_rows_grad, over_nodes, preferred_element_type=jnp.float32
    )
    value_term = lax.dot_general(
        node_states, value_rows_grad, over_nodes, preferred_element_type=jnp.float32
    )
    query_grad, key_grad, value_grad = (
        lax.psum_scatter(
            query_term.astype(jnp.bfloat16), "col", scatter_dimension=0, tiled=True
        ).astype(jnp.float32),
        lax.psum_scatter(
            key_term.astype(jnp.bfloat16), "col", scatter_dimension=0, tiled=True
        ).astype(jnp.float32),
        lax.psum_scatter(
            value_term.astype(jnp.bfloat16), "col", scatter_dimension=0, tiled=True
        ).astype(jnp.float32),
    )
    return (attended, node_grad, query_grad, key_grad, value_grad)


MESH = pl.DeviceIdType.MESH
GROUP = 4
CUTS = 2


def meet(axes):
    barrier = pltpu.get_barrier_semaphore()
    total = 0
    for axis, count in axes:
        me = lax.axis_index(axis)
        for step in range(1, count):
            peer = lax.rem(me + step, count)
            pl.semaphore_signal(barrier, inc=1, device_id={axis: peer}, device_id_type=MESH)
            total += 1
    pl.semaphore_wait(barrier, total)


def spread_kernel(
    n, x_ref, wq_ref, wk_ref, wv_ref, grad_ref, code_ref, heads_ref, codes_ref, x_out,
    x_all, keep_sem, grads, weights, weight, outbox, inbox, load_sem, grad_send, grad_recv, code_send, code_recv,
    chain_send, chain_recv, core_send, core_recv, row_send, row_recv,
):
    me = lax.axis_index("col")
    half = lax.axis_index("row")
    other = 1 - half
    near = n // 2
    z = lax.div(me, 2)
    k = lax.rem(me, 2)
    twin = 2 * z + 1 - k

    loads = [
        pltpu.make_async_copy(
            ref.at[:, pl.ds(pl.multiple_of(z * 2 * DH, 2 * DH), 2 * DH)],
            weights.at[i],
            load_sem.at[i],
        )
        for i, ref in enumerate((wq_ref, wk_ref, wv_ref))
    ]
    loads.append(pltpu.make_async_copy(grad_ref, grads, load_sem.at[3]))
    loads.append(pltpu.make_async_copy(x_ref, x_all.at[me], load_sem.at[4]))
    loads.append(pltpu.make_async_copy(code_ref, codes_ref.at[me], load_sem.at[5]))
    for load in loads:
        load.start()
    meet([("col", n), ("row", 2)])

    def code_copy(peer, slot):
        return pltpu.make_async_remote_copy(
            src_ref=code_ref, dst_ref=codes_ref.at[slot], send_sem=code_send.at[peer],
            recv_sem=code_recv.at[slot], device_id={"col": peer}, device_id_type=MESH,
        )

    def grad_copy(peer, slot):
        return pltpu.make_async_remote_copy(
            src_ref=outbox.at[peer], dst_ref=inbox.at[slot], send_sem=grad_send.at[peer],
            recv_sem=grad_recv.at[slot], device_id={"col": peer}, device_id_type=MESH,
        )

    def chain_copy(src, origin, cut, side, target):
        return pltpu.make_async_remote_copy(
            src_ref=src, dst_ref=x_all.at[2 * origin + k, half * CUTS + cut],
            send_sem=chain_send.at[side, origin, cut], recv_sem=chain_recv.at[origin, cut],
            device_id={"col": 2 * target + k}, device_id_type=MESH,
        )

    def core_copy(src, origin, part, core):
        return pltpu.make_async_remote_copy(
            src_ref=src, dst_ref=x_all.at[2 * origin + core, part],
            send_sem=core_send.at[origin, part], recv_sem=core_recv.at[origin, part],
            device_id={"col": twin}, device_id_type=MESH,
        )

    def row_copy(src, origin, cut, part):
        return pltpu.make_async_remote_copy(
            src_ref=src, dst_ref=x_all.at[2 * origin + k, part * CUTS + cut],
            send_sem=row_send.at[origin, cut], recv_sem=row_recv.at[origin, cut],
            device_id={"row": other}, device_id_type=MESH,
        )

    peers = [lax.rem(me + step, n) for step in range(1, n)]
    up, down = z + 1 < near, z >= 1

    for cut in range(CUTS):
        piece = x_ref.at[half * CUTS + cut]

        @pl.when(up)
        def _(piece=piece, cut=cut):
            chain_copy(piece, z, cut, 0, z + 1).start()

        @pl.when(down)
        def _(piece=piece, cut=cut):
            chain_copy(piece, z, cut, 1, z - 1).start()

    for part in range(2 * CUTS):
        core_copy(x_ref.at[part], z, part, k).start()
    for peer in peers:
        code_copy(peer, me).start()
    loads[3].wait()
    deep = grads.shape[0] // 2
    for head in range(n):
        cols = slice(head * DH, (head + 1) * DH)
        outbox[head] = jnp.concatenate([grads[:deep, cols], grads[deep:, cols]], axis=1)
    for peer in peers:
        grad_copy(peer, me).start()
    inbox[me] = outbox[me]
    for load in loads[:3] + loads[4:]:
        load.wait()
    factor = 1.0 / math.sqrt(DH)
    picked = [
        jnp.where(k == 0, weights[i, :, :DH], weights[i, :, DH:]) for i in range(3)
    ]
    for place, i in enumerate((0, 0, 1, 2)):
        weight[:, place * DH : (place + 1) * DH] = picked[i]

    def keep(origin):
        pair = pl.ds(2 * origin, 2)
        return pltpu.make_async_copy(x_all.at[pair], x_out.at[pair], keep_sem.at[origin])

    def project(origin):
        for part in range(2 * CUTS):
            core_copy(x_all.at[2 * origin + 1 - k, part], origin, part, 1 - k).wait_recv()
        keep(origin).start()
        for core in range(2):
            panel = 2 * origin + core
            x = x_all[panel].reshape(2 * deep, x_all.shape[3])
            made = jnp.dot(x, weight[...], preferred_element_type=jnp.float32)
            made = made.astype(jnp.bfloat16)
            queries = (made[:, :DH].astype(jnp.float32) * factor).astype(jnp.bfloat16)
            heads_ref[panel, :, :DH] = queries
            heads_ref[panel, :, 2 * DH :] = made[:, 2 * DH :]

    def through_row(origin, cut, there):
        @pl.when(there)
        def _():
            block = x_all.at[2 * origin + k, other * CUTS + cut]
            row_copy(block, origin, cut, other).wait_recv()
            core_copy(block, origin, other * CUTS + cut, k).start()

    def onto(origin, cut, there, onward, side, target):
        @pl.when(there)
        def _():
            block = x_all.at[2 * origin + k, half * CUTS + cut]
            chain_copy(block, origin, cut, side, z).wait_recv()

            @pl.when(onward)
            def _():
                chain_copy(block, origin, cut, side, target).start()

            row_copy(block, origin, cut, half).start()
            core_copy(block, origin, half * CUTS + cut, k).start()

    steps = []
    for d in range(1, near):
        for cut in range(CUTS):
            steps.append((z - d, cut, z - d >= 0, up, 0, z + 1))
            steps.append((z + d, cut, z + d < near, down, 1, z - 1))
    each = 2 * CUTS
    for step, (origin, cut, there, onward, side, target) in enumerate(steps):
        onto(origin, cut, there, onward, side, target)
        if step >= 2:
            through_row(*steps[step - 2][:3])
        if step == each - 1:
            project(z)
        if step == each + 1:
            for peer in peers:
                grad_copy(peer, peer).wait_recv()
            for panel in range(n):
                heads_ref[panel, :deep, DH : 2 * DH] = inbox[panel, :, :DH]
                heads_ref[panel, deep:, DH : 2 * DH] = inbox[panel, :, DH:]
        if step >= 2 * each - 1 and (step + 1) % each == 0:
            for origin, _, there, _, _, _ in steps[step - 2 * each + 1 : step - 2 * each + 3]:
                pl.when(there)(functools.partial(project, origin))
    for origin, cut, there, _, _, _ in steps[-2:]:
        through_row(origin, cut, there)
    for origin, _, there, _, _, _ in steps[-2:]:
        pl.when(there)(functools.partial(project, origin))
    for peer in peers:
        code_copy(peer, peer).wait_recv()
    for origin in range(near):
        keep(origin).wait()
    for peer in peers:
        code_copy(peer, me).wait_send()
        grad_copy(peer, me).wait_send()
    for cut in range(CUTS):
        piece = x_ref.at[half * CUTS + cut]

        @pl.when(up)
        def _(piece=piece, cut=cut):
            chain_copy(piece, z, cut, 0, z + 1).wait_send()

        @pl.when(down)
        def _(piece=piece, cut=cut):
            chain_copy(piece, z, cut, 1, z - 1).wait_send()

    for part in range(2 * CUTS):
        core_copy(x_ref.at[part], z, part, k).wait_send()
    for origin, cut, there, onward, side, target in steps:
        @pl.when(there)
        def _(origin=origin, cut=cut, onward=onward, side=side, target=target):
            block = x_all.at[2 * origin + k, half * CUTS + cut]

            @pl.when(onward)
            def _():
                chain_copy(block, origin, cut, side, target).wait_send()

            row_copy(block, origin, cut, half).wait_send()
            core_copy(block, origin, half * CUTS + cut, k).wait_send()
            core_copy(
                x_all.at[2 * origin + k, other * CUTS + cut], origin, other * CUTS + cut, k
            ).wait_send()


def spread(node_states, query_weight, key_weight, value_weight, output_grad, codes, n):
    rows, depth = node_states.shape
    width = 4 * DH
    near = n // 2
    vmem = pl.BlockSpec(memory_space=pltpu.VMEM)
    hbm = pl.BlockSpec(memory_space=pltpu.HBM)
    dma = pltpu.SemaphoreType.DMA
    return pl.pallas_call(
        functools.partial(spread_kernel, n),
        out_shape=(
            jax.ShapeDtypeStruct((n, rows, width), jnp.bfloat16),
            jax.ShapeDtypeStruct((n,) + codes.shape, jnp.int32),
            jax.ShapeDtypeStruct((n, 2 * CUTS, rows // (2 * CUTS), depth), jnp.bfloat16),
        ),
        in_specs=[hbm] * 5 + [vmem],
        out_specs=(vmem, vmem, hbm),
        scratch_shapes=[
            pltpu.VMEM((n, 2 * CUTS, rows // (2 * CUTS), depth), jnp.bfloat16),
            dma((near,)),
            pltpu.VMEM(output_grad.shape, jnp.bfloat16),
            pltpu.VMEM((3, depth, 2 * DH), jnp.bfloat16),
            pltpu.VMEM((depth, 4 * DH), jnp.bfloat16),
            pltpu.VMEM((n, rows // 2, 2 * DH), jnp.bfloat16),
            pltpu.VMEM((n, rows // 2, 2 * DH), jnp.bfloat16),
            dma((6,)), dma((n,)), dma((n,)), dma((n,)), dma((n,)),
            dma((2, near, CUTS)), dma((near, CUTS)), dma((near, 2 * CUTS)),
            dma((near, 2 * CUTS)), dma((near, CUTS)), dma((near, CUTS)),
        ],
        compiler_params=pltpu.CompilerParams(
            collective_id=0, has_side_effects=True, vmem_limit_bytes=54 << 20
        ),
        cost_estimate=pl.CostEstimate(
            flops=6 * rows * depth * n * DH, bytes_accessed=40 << 20, transcendentals=0
        ),
        name="spread_heads",
    )(
        node_states.reshape(2 * CUTS, rows // (2 * CUTS), depth), query_weight, key_weight, value_weight,
        output_grad, codes,
    )


def attend_kernel(
    n, blocks, codes_ref, heads_ref, out_ref, pairs_acc, scores_buf, grads_buf, found, counts
):
    lanes = lax.broadcasted_iota(jnp.int32, (BLK, 2 * DH), 1)
    first = lanes < DH
    key_total = n * blocks
    nt = (((1,), (1,)), ((), ()))
    pairs_acc[...] = jnp.zeros_like(pairs_acc)

    def collect(panel):
        for q in range(blocks):
            counts[q] = 0
            for k in range(key_total):
                found[q, k] = 0
        total = codes_ref[panel, 2, 0]

        def one(slot, carry):
            q = codes_ref[panel, 0, slot]
            place = counts[q]
            found[q, place] = codes_ref[panel, 1, slot]
            counts[q] = place + 1
            return carry

        lax.fori_loop(0, total, one, 0)

    def work(panel, groups):
        width = GROUP * BLK
        stacks = []
        for q in range(blocks):
            both = heads_ref[panel, q * BLK : (q + 1) * BLK, : 2 * DH]
            zero = jnp.zeros_like(both)
            stacks.append(
                jnp.concatenate([jnp.where(first, both, zero), jnp.where(first, zero, both)], axis=0)
            )

        def table(q, g):
            parts = []
            for j in range(GROUP):
                k = found[q, g * GROUP + j]
                start = pl.multiple_of(lax.rem(k, blocks) * BLK, BLK)
                parts.append(heads_ref[lax.div(k, blocks), pl.ds(start, BLK), 2 * DH :])
            return jnp.concatenate(parts, axis=0)

        tops, totals, outs, deltas = [], [], [], []
        for q in range(blocks):
            top = jnp.full((BLK, BLK), LOWEST, jnp.float32)
            for g in range(groups):
                both = lax.dot_general(stacks[q], table(q, g), nt, preferred_element_type=jnp.float32)
                grads_buf[q, g] = both[BLK:]
                for j in range(GROUP):
                    tile = both[:BLK, j * BLK : (j + 1) * BLK]
                    live = g * GROUP + j < counts[q]
                    tile = jnp.where(live, tile, LOWEST)
                    scores_buf[q, g, :, j * BLK : (j + 1) * BLK] = tile
                    top = jnp.maximum(top, tile)
            tops.append(jnp.max(top, axis=1, keepdims=True))
        for q in range(blocks):
            total = jnp.zeros((BLK, BLK), jnp.float32)
            for g in range(groups):
                terms = jnp.exp(scores_buf[q, g] - tops[q])
                scores_buf[q, g] = terms
                for j in range(GROUP):
                    total = total + terms[:, j * BLK : (j + 1) * BLK]
            totals.append(1.0 / jnp.sum(total, axis=1, keepdims=True))
        for q in range(blocks):
            out = jnp.zeros((BLK, 2 * DH), jnp.float32)
            for g in range(groups):
                weights = (scores_buf[q, g] * totals[q]).astype(jnp.bfloat16)
                out = out + jnp.dot(weights, table(q, g), preferred_element_type=jnp.float32)
            outs.append(out)
            grad = stacks[q][BLK:].astype(jnp.float32)
            deltas.append(jnp.sum(grad * out, axis=1, keepdims=True))
        for q in range(blocks):
            rows_grad = jnp.zeros((BLK, 2 * DH), jnp.float32)
            turned = stacks[q].T
            for g in range(groups):
                weights = (scores_buf[q, g] * totals[q]).astype(jnp.bfloat16)
                score_grad = (
                    weights.astype(jnp.float32) * (grads_buf[q, g] - deltas[q])
                ).astype(jnp.bfloat16)
                rows_grad = rows_grad + jnp.dot(
                    score_grad, table(q, g), preferred_element_type=jnp.float32
                )
                pair = jnp.dot(
                    turned,
                    jnp.concatenate([score_grad, weights], axis=0),
                    preferred_element_type=jnp.float32,
                )
                for j in range(GROUP):
                    k = found[q, g * GROUP + j]
                    pairs_acc[k] = pairs_acc[k] + pair[:, j * BLK : (j + 1) * BLK]
            factor = 1.0 / math.sqrt(DH)
            out_ref[panel, q * BLK : (q + 1) * BLK, : 2 * DH] = jnp.where(
                first, rows_grad * factor, outs[q]
            ).astype(jnp.bfloat16)

    def one_panel(panel, carry):
        collect(panel)
        most = counts[0]
        for q in range(1, blocks):
            most = jnp.maximum(most, counts[q])
        groups = lax.div(most + (GROUP - 1), GROUP)
        for size in range(1, key_total // GROUP + 1):
            pl.when(groups == size)(functools.partial(work, panel, size))
        return carry

    lax.fori_loop(0, n, one_panel, 0)
    for k in range(key_total):
        row = (k % blocks) * BLK
        out_ref[k // blocks, row : row + BLK, 2 * DH :] = pairs_acc[k].T.astype(jnp.bfloat16)


def attend(heads, codes, n, blocks):
    key_total = n * blocks
    groups = key_total // GROUP
    tiles = key_total * key_total
    return pl.pallas_call(
        functools.partial(attend_kernel, n, blocks),
        out_shape=jax.ShapeDtypeStruct(heads.shape, jnp.bfloat16),
        in_specs=[
            pl.BlockSpec(memory_space=pltpu.SMEM),
            pl.BlockSpec(memory_space=pltpu.VMEM),
        ],
        out_specs=pl.BlockSpec(memory_space=pltpu.VMEM),
        scratch_shapes=[
            pltpu.VMEM((key_total, 2 * DH, BLK), jnp.float32),
            pltpu.VMEM((blocks, groups, BLK, GROUP * BLK), jnp.float32),
            pltpu.VMEM((blocks, groups, BLK, GROUP * BLK), jnp.float32),
            pltpu.SMEM((blocks, key_total), jnp.int32),
            pltpu.SMEM((blocks,), jnp.int32),
        ],
        compiler_params=pltpu.CompilerParams(vmem_limit_bytes=16 << 20),
        cost_estimate=pl.CostEstimate(
            flops=tiles * 24 * BLK * BLK * DH, bytes_accessed=80 << 20,
            transcendentals=tiles * BLK * BLK,
        ),
        name="attend_heads",
    )(codes, heads)


def collect_kernel(
    n, n_row, res_ref, x_ref, wq_ref, wk_ref, wv_ref,
    att_ref, terms_in, part_in,
    inbox, terms_out, part_out,
    send_sem, recv_sem, term_send, term_recv, row_send, row_recv,
):
    me = lax.axis_index("col")
    my_row = lax.axis_index("row")
    meet([("col", n), ("row", n_row)])
    peers = [lax.rem(me + step, n) for step in range(1, n)]
    row_peers = [lax.rem(my_row + step, n_row) for step in range(1, n_row)]
    cols = part_out.shape[2]

    def res_copy(peer, slot):
        return pltpu.make_async_remote_copy(
            src_ref=res_ref.at[peer], dst_ref=inbox.at[slot], send_sem=send_sem.at[peer],
            recv_sem=recv_sem.at[slot], device_id={"col": peer}, device_id_type=MESH,
        )

    def term_copy(peer, slot):
        return pltpu.make_async_remote_copy(
            src_ref=terms_out.at[peer], dst_ref=terms_in.at[slot], send_sem=term_send.at[peer],
            recv_sem=term_recv.at[slot], device_id={"col": peer}, device_id_type=MESH,
        )

    def row_copy(peer, slot):
        return pltpu.make_async_remote_copy(
            src_ref=part_out.at[peer], dst_ref=part_in.at[slot], send_sem=row_send.at[peer],
            recv_sem=row_recv.at[slot], device_id={"row": peer}, device_id_type=MESH,
        )

    for peer in peers:
        res_copy(peer, me).start()
    inbox[me] = res_ref[me]
    rows = res_ref.shape[1]
    depth = x_ref.shape[3]
    chunk = depth // n
    turned = res_ref[...].reshape(n * rows, 4 * DH).T
    for peer in range(n):
        term = jnp.dot(
            turned,
            x_ref[:, :, :, peer * chunk : (peer + 1) * chunk].reshape(n * rows, chunk),
            preferred_element_type=jnp.float32,
        ).astype(jnp.bfloat16)
        terms_out[peer, :DH] = term[:DH]
        terms_out[peer, DH:] = term[2 * DH :]
    terms_in[me] = terms_out[me]
    for peer in peers:
        res_copy(peer, peer).wait_recv()
    for peer in peers:
        term_copy(peer, me).start()

    def piece(which):
        return jnp.concatenate(
            [inbox[h, :, which * DH : (which + 1) * DH] for h in range(n)], axis=1
        )

    nt = (((1,), (1,)), ((), ()))
    grads = [piece(0), piece(2), piece(3)]
    weights = [wq_ref, wk_ref, wv_ref]
    for r in range(n_row):
        span = slice(r * cols, (r + 1) * cols)
        part = jnp.zeros((rows, cols), jnp.float32)
        for grad, weight in zip(grads, weights):
            part = part + lax.dot_general(
                grad, weight[span, :], nt, preferred_element_type=jnp.float32
            )
        part_out[r] = part.astype(jnp.bfloat16)
    for peer in row_peers:
        row_copy(peer, my_row).start()
    att_ref[...] = piece(1)
    for peer in peers:
        term_copy(peer, peer).wait_recv()
    part_in[my_row] = part_out[my_row]
    for peer in row_peers:
        row_copy(peer, peer).wait_recv()
    for peer in peers:
        res_copy(peer, me).wait_send()
        term_copy(peer, me).wait_send()
    for peer in row_peers:
        row_copy(peer, my_row).wait_send()


def finish_kernel(
    n, n_row, att_in, terms, parts, att_ref, node_ref, qg_ref, kg_ref, vg_ref,
    node_buf, grad_buf, sem,
):
    copies = [pltpu.make_async_copy(att_in, att_ref, sem.at[0])]
    copies[0].start()
    total = parts[0].astype(jnp.float32)
    for r in range(1, n_row):
        total = total + parts[r].astype(jnp.float32)
    node_buf[...] = total
    copies.append(pltpu.make_async_copy(node_buf, node_ref, sem.at[1]))
    copies[1].start()
    for which, ref in enumerate((qg_ref, kg_ref, vg_ref)):
        for h in range(0, n, 2):
            pair = jnp.concatenate(
                [
                    terms[h, which * DH : (which + 1) * DH],
                    terms[h + 1, which * DH : (which + 1) * DH],
                ],
                axis=0,
            )
            grad_buf[which, :, h * DH : (h + 2) * DH] = pair.astype(jnp.float32).T
        copies.append(pltpu.make_async_copy(grad_buf.at[which], ref, sem.at[2 + which]))
        copies[-1].start()
    for copy in copies:
        copy.wait()


def collect_grads(res, x_all, query_weight, key_weight, value_weight, n, n_row):
    rows = res.shape[1]
    depth = x_all.shape[3]
    cols = depth // n_row
    chunk = depth // n
    head_cols = n * DH
    vmem = pl.BlockSpec(memory_space=pltpu.VMEM)
    hbm = pl.BlockSpec(memory_space=pltpu.HBM)
    dma = pltpu.SemaphoreType.DMA
    att, terms, parts = pl.pallas_call(
        functools.partial(collect_kernel, n, n_row),
        out_shape=(
            jax.ShapeDtypeStruct((rows, head_cols), jnp.bfloat16),
            jax.ShapeDtypeStruct((n, 3 * DH, chunk), jnp.bfloat16),
            jax.ShapeDtypeStruct((n_row, rows, cols), jnp.bfloat16),
        ),
        in_specs=[vmem] * 5,
        out_specs=(vmem,) * 3,
        scratch_shapes=[
            pltpu.VMEM(res.shape, jnp.bfloat16),
            pltpu.VMEM((n, 3 * DH, chunk), jnp.bfloat16),
            pltpu.VMEM((n_row, rows, cols), jnp.bfloat16),
            dma((n,)), dma((n,)), dma((n,)), dma((n,)), dma((n_row,)), dma((n_row,)),
        ],
        compiler_params=pltpu.CompilerParams(
            collective_id=1, has_side_effects=True, vmem_limit_bytes=20 << 20
        ),
        name="collect_grads",
    )(res, x_all, query_weight, key_weight, value_weight)
    return pl.pallas_call(
        functools.partial(finish_kernel, n, n_row),
        out_shape=(
            jax.ShapeDtypeStruct((rows, head_cols), jnp.bfloat16),
            jax.ShapeDtypeStruct((rows, cols), jnp.float32),
            jax.ShapeDtypeStruct((chunk, head_cols), jnp.float32),
            jax.ShapeDtypeStruct((chunk, head_cols), jnp.float32),
            jax.ShapeDtypeStruct((chunk, head_cols), jnp.float32),
        ),
        in_specs=[vmem] * 3,
        out_specs=(hbm,) * 5,
        scratch_shapes=[
            pltpu.VMEM((rows, cols), jnp.float32),
            pltpu.VMEM((3, chunk, head_cols), jnp.float32),
            dma((5,)),
        ],
        compiler_params=pltpu.CompilerParams(vmem_limit_bytes=16 << 20),
        name="finish",
    )(att, terms, parts)


def per_device_heads(
    n, n_row, node_states, query_weight, key_weight, value_weight, output_grad, pair_list, pair_count
):
    blocks = node_states.shape[0] // BLK
    slots = pair_list.shape[1]
    listed = jnp.pad(pair_list[0].T, ((0, 0), (0, BLK - slots)))
    total = jnp.broadcast_to(pair_count[0], (6, BLK))
    codes = jnp.concatenate([listed, total], axis=0)
    heads, codes_all, x_all = spread(
        node_states, query_weight, key_weight, value_weight, output_grad, codes, n
    )
    res = attend(heads, codes_all, n, blocks)
    return collect_grads(res, x_all, query_weight, key_weight, value_weight, n, n_row)


def per_device(mesh, *arrays):
    n, n_row = mesh.shape["col"], mesh.shape["row"]
    node_states, query_weight, pair_list = arrays[0], arrays[1], arrays[5]
    blocks = node_states.shape[0] // BLK
    one_head_each = query_weight.shape[1] == n * DH and n % 2 == 0 and n_row == 2
    tiled = (n * blocks) % GROUP == 0 and pair_list.shape[1] <= BLK
    lanes = node_states.shape[1] % (n * BLK) == 0 and node_states.shape[1] % (n_row * BLK) == 0
    if one_head_each and tiled and lanes:
        return per_device_heads(n, n_row, *arrays)
    return per_device_slots(*arrays)


def solution(mesh):
    return jax.shard_map(
        functools.partial(per_device, mesh),
        mesh=mesh,
        in_specs=(
            P(("groups", "col"), None),
            P(None, "row"),
            P(None, "row"),
            P(None, "row"),
            P(("groups", "col"), "row"),
            P(("groups", "col"), None, None),
            P(("groups", "col")),
        ),
        out_specs=(
            P(("groups", "col"), "row"),
            P(("groups", "col"), "row"),
            P(("groups", "col"), "row"),
            P(("groups", "col"), "row"),
            P(("groups", "col"), "row"),
        ),
        check_vma=False,
    )
```

```python
import functools
import math

import jax
import jax.numpy as jnp
from jax import lax
from jax.experimental import pallas as pl
from jax.experimental.pallas import tpu as pltpu
from jax.sharding import PartitionSpec as P

DH = 64
BLK = 128


LOWEST = -1e30
EXACT = lax.Precision.HIGHEST


def slot_batch(pair_rows, pair_total, turn_index, width, blocks):
    start = turn_index * width
    query_block = pair_rows[:, 0]
    key_block = pair_rows[:, 1]
    slot_live = start + jnp.arange(width, dtype=jnp.int32) < pair_total
    owners = jnp.logical_and(
        query_block[:, None] == jnp.arange(blocks, dtype=jnp.int32)[None, :], slot_live[:, None]
    )
    return (query_block, key_block, slot_live, owners)


def batch_tiles(query_tiles, table_tiles, query_block, key_block, head_cols, factor):
    head_count = head_cols // DH
    width = query_block.shape[0]
    query_pick = jnp.take(query_tiles, query_block, axis=0)
    table_pick = jnp.take(table_tiles, key_block, axis=0)
    key_pick = table_pick[:, :, :head_cols].reshape(width, BLK, head_count, DH)
    value_pick = table_pick[:, :, head_cols:].reshape(width, BLK, head_count, DH)
    scores = (
        jnp.einsum("sihd,sjhd->shij", query_pick, key_pick, preferred_element_type=jnp.float32)
        * factor
    )
    return (query_pick, key_pick, value_pick, scores)


def batch_weights(scores, row_top, totals, query_block, slot_live):
    top_pick = jnp.take(row_top, query_block, axis=0)
    total_pick = jnp.take(totals, query_block, axis=0)
    weights = jnp.exp(scores - top_pick[..., None]) / total_pick[..., None]
    return jnp.where(slot_live[:, None, None, None], weights, 0.0).astype(jnp.bfloat16)


def per_device_slots(
    node_states, query_weight, key_weight, value_weight, output_grad, pair_list, pair_count
):
    head_cols = query_weight.shape[1]
    head_count = head_cols // DH
    panel_rows = node_states.shape[0]
    blocks = panel_rows // BLK
    factor = 1.0 / math.sqrt(DH)
    pair_rows = pair_list[0]
    pair_total = pair_count[0]
    width = math.gcd(pair_rows.shape[0], 32)
    turns = (pair_total + width - 1) // width
    queries = jnp.dot(node_states, query_weight, preferred_element_type=jnp.float32).astype(
        jnp.bfloat16
    )
    keys_here = jnp.dot(node_states, key_weight, preferred_element_type=jnp.float32).astype(
        jnp.bfloat16
    )
    values_here = jnp.dot(node_states, value_weight, preferred_element_type=jnp.float32).astype(
        jnp.bfloat16
    )
    local_table = jnp.concatenate([keys_here, values_here], axis=1)
    key_table = lax.all_gather(local_table, "col", axis=0, tiled=True)
    key_blocks_all = key_table.shape[0] // BLK
    query_tiles = queries.reshape(blocks, BLK, head_count, DH)
    table_tiles = key_table.reshape(key_blocks_all, BLK, 2 * head_cols)

    def stats_turn(turn_index, state_pair):
        row_top, totals = state_pair
        query_block, key_block, slot_live, owners = slot_batch(
            pair_rows, pair_total, turn_index, width, blocks
        )
        scores = batch_tiles(query_tiles, table_tiles, query_block, key_block, head_cols, factor)[3]
        pair_top = jnp.max(scores, axis=3)
        block_top = jnp.max(jnp.where(owners[:, :, None, None], pair_top[:, None], LOWEST), axis=0)
        new_top = jnp.maximum(row_top, block_top)
        top_pick = jnp.take(new_top, query_block, axis=0)
        exp_terms = jnp.where(
            slot_live[:, None, None, None], jnp.exp(scores - top_pick[..., None]), 0.0
        )
        added = jnp.einsum(
            "sn,shi->nhi", owners.astype(jnp.float32), jnp.sum(exp_terms, axis=3), precision=EXACT
        )
        totals = totals * jnp.exp(row_top - new_top) + added
        return (new_top, totals)

    start_top = jnp.full((blocks, head_count, BLK), LOWEST, jnp.float32)
    start_total = jnp.zeros((blocks, head_count, BLK), jnp.float32)
    row_top, totals = lax.fori_loop(0, turns, stats_turn, (start_top, start_total))

    def attend_turn(turn_index, output):
        query_block, key_block, slot_live, owners = slot_batch(
            pair_rows, pair_total, turn_index, width, blocks
        )
        query_pick, key_pick, value_pick, scores = batch_tiles(
            query_tiles, table_tiles, query_block, key_block, head_cols, factor
        )
        weights = batch_weights(scores, row_top, totals, query_block, slot_live)
        update = jnp.einsum(
            "shij,sjhd->sihd", weights, value_pick, preferred_element_type=jnp.float32
        )
        return output + jnp.einsum(
            "sn,sihd->nihd", owners.astype(jnp.float32), update, precision=EXACT
        )

    output = lax.fori_loop(
        0, turns, attend_turn, jnp.zeros((blocks, BLK, head_count, DH), jnp.float32)
    )
    attended = output.reshape(panel_rows, head_cols).astype(jnp.bfloat16)
    grad_tiles = output_grad.reshape(blocks, BLK, head_count, DH)
    deltas = jnp.sum(grad_tiles.astype(jnp.float32) * output, axis=3)
    back_table = lax.all_gather(local_table, "col", axis=0, tiled=True)
    back_tiles = back_table.reshape(key_blocks_all, BLK, 2 * head_cols)

    def backward_turn(turn_index, state_pair):
        grad_rows, key_grads = state_pair
        query_block, key_block, slot_live, owners = slot_batch(
            pair_rows, pair_total, turn_index, width, blocks
        )
        query_pick, key_pick, value_pick, scores = batch_tiles(
            query_tiles, back_tiles, query_block, key_block, head_cols, factor
        )
        weights = batch_weights(scores, row_top, totals, query_block, slot_live)
        grad_pick = jnp.take(grad_tiles, query_block, axis=0)
        value_part = jnp.einsum(
            "shij,sihd->sjhd", weights, grad_pick, preferred_element_type=jnp.float32
        )
        prob_grad = jnp.einsum(
            "sihd,sjhd->shij", grad_pick, value_pick, preferred_element_type=jnp.float32
        )
        delta_pick = jnp.transpose(jnp.take(deltas, query_block, axis=0), (0, 2, 1))
        score_grad = (weights.astype(jnp.float32) * (prob_grad - delta_pick[..., None])).astype(
            jnp.bfloat16
        )
        query_part = (
            jnp.einsum("shij,sjhd->sihd", score_grad, key_pick, preferred_element_type=jnp.float32)
            * factor
        )
        key_part = (
            jnp.einsum(
                "shij,sihd->sjhd", score_grad, query_pick, preferred_element_type=jnp.float32
            )
            * factor
        )
        grad_rows = grad_rows + jnp.einsum(
            "sn,sihd->nihd", owners.astype(jnp.float32), query_part, precision=EXACT
        )
        rows_update = jnp.concatenate(
            [key_part.reshape(width, BLK, head_cols), value_part.reshape(width, BLK, head_cols)],
            axis=2,
        )
        key_grads = key_grads + jax.ops.segment_sum(
            rows_update, key_block, num_segments=key_blocks_all
        )
        return (grad_rows, key_grads)

    start_rows = jnp.zeros((blocks, BLK, head_count, DH), jnp.float32)
    start_keys = jnp.zeros((key_blocks_all, BLK, 2 * head_cols), jnp.float32)
    grad_rows, key_grads = lax.fori_loop(0, turns, backward_turn, (start_rows, start_keys))
    key_grads = key_grads.reshape(key_blocks_all * BLK, 2 * head_cols)
    pair_grads = lax.psum_scatter(
        key_grads.astype(jnp.bfloat16), "col", scatter_dimension=0, tiled=True
    ).astype(jnp.float32)
    query_rows_grad = grad_rows.reshape(panel_rows, head_cols).astype(jnp.bfloat16)
    key_rows_grad = pair_grads[:, :head_cols].astype(jnp.bfloat16)
    value_rows_grad = pair_grads[:, head_cols:].astype(jnp.bfloat16)
    contract = (((1,), (1,)), ((), ()))
    partial_sum = lax.dot_general(
        query_rows_grad, query_weight, contract, preferred_element_type=jnp.float32
    )
    partial_sum = partial_sum + lax.dot_general(
        key_rows_grad, key_weight, contract, preferred_element_type=jnp.float32
    )
    partial_sum = partial_sum + lax.dot_general(
        value_rows_grad, value_weight, contract, preferred_element_type=jnp.float32
    )
    node_grad = lax.psum_scatter(
        partial_sum.astype(jnp.bfloat16), "row", scatter_dimension=1, tiled=True
    ).astype(jnp.float32)
    over_nodes = (((0,), (0,)), ((), ()))
    query_term = lax.dot_general(
        node_states, query_rows_grad, over_nodes, preferred_element_type=jnp.float32
    )
    key_term = lax.dot_general(
        node_states, key_rows_grad, over_nodes, preferred_element_type=jnp.float32
    )
    value_term = lax.dot_general(
        node_states, value_rows_grad, over_nodes, preferred_element_type=jnp.float32
    )
    query_grad, key_grad, value_grad = (
        lax.psum_scatter(
            query_term.astype(jnp.bfloat16), "col", scatter_dimension=0, tiled=True
        ).astype(jnp.float32),
        lax.psum_scatter(
            key_term.astype(jnp.bfloat16), "col", scatter_dimension=0, tiled=True
        ).astype(jnp.float32),
        lax.psum_scatter(
            value_term.astype(jnp.bfloat16), "col", scatter_dimension=0, tiled=True
        ).astype(jnp.float32),
    )
    return (attended, node_grad, query_grad, key_grad, value_grad)


MESH = pl.DeviceIdType.MESH
GROUP = 2
CUTS = 2


def meet(axes):
    barrier = pltpu.get_barrier_semaphore()
    total = 0
    for axis, count in axes:
        me = lax.axis_index(axis)
        for step in range(1, count):
            peer = lax.rem(me + step, count)
            pl.semaphore_signal(barrier, inc=1, device_id={axis: peer}, device_id_type=MESH)
            total += 1
    pl.semaphore_wait(barrier, total)


def spread_kernel(
    n, x_ref, wq_ref, wk_ref, wv_ref, grad_ref, code_ref, heads_ref, codes_ref, x_out,
    x_all, keep_sem, grads, weights, weight, outbox, inbox, load_sem, grad_send, grad_recv, code_send, code_recv,
    chain_send, chain_recv, core_send, core_recv, row_send, row_recv,
):
    me = lax.axis_index("col")
    half = lax.axis_index("row")
    other = 1 - half
    near = n // 2
    z = lax.div(me, 2)
    k = lax.rem(me, 2)
    twin = 2 * z + 1 - k

    loads = [
        pltpu.make_async_copy(
            ref.at[:, pl.ds(pl.multiple_of(z * 2 * DH, 2 * DH), 2 * DH)],
            weights.at[i],
            load_sem.at[i],
        )
        for i, ref in enumerate((wq_ref, wk_ref, wv_ref))
    ]
    loads.append(pltpu.make_async_copy(grad_ref, grads, load_sem.at[3]))
    loads.append(pltpu.make_async_copy(x_ref, x_all.at[me], load_sem.at[4]))
    loads.append(pltpu.make_async_copy(code_ref, codes_ref.at[me], load_sem.at[5]))
    for load in loads:
        load.start()
    meet([("col", n), ("row", 2)])

    def code_copy(peer, slot):
        return pltpu.make_async_remote_copy(
            src_ref=code_ref, dst_ref=codes_ref.at[slot], send_sem=code_send.at[peer],
            recv_sem=code_recv.at[slot], device_id={"col": peer}, device_id_type=MESH,
        )

    def grad_copy(peer, slot):
        return pltpu.make_async_remote_copy(
            src_ref=outbox.at[peer], dst_ref=inbox.at[slot], send_sem=grad_send.at[peer],
            recv_sem=grad_recv.at[slot], device_id={"col": peer}, device_id_type=MESH,
        )

    def chain_copy(src, origin, cut, side, target):
        return pltpu.make_async_remote_copy(
            src_ref=src, dst_ref=x_all.at[2 * origin + k, half * CUTS + cut],
            send_sem=chain_send.at[side, origin, cut], recv_sem=chain_recv.at[origin, cut],
            device_id={"col": 2 * target + k}, device_id_type=MESH,
        )

    def core_copy(src, origin, part, core):
        return pltpu.make_async_remote_copy(
            src_ref=src, dst_ref=x_all.at[2 * origin + core, part],
            send_sem=core_send.at[origin, part], recv_sem=core_recv.at[origin, part],
            device_id={"col": twin}, device_id_type=MESH,
        )

    def row_copy(src, origin, cut, part):
        return pltpu.make_async_remote_copy(
            src_ref=src, dst_ref=x_all.at[2 * origin + k, part * CUTS + cut],
            send_sem=row_send.at[origin, cut], recv_sem=row_recv.at[origin, cut],
            device_id={"row": other}, device_id_type=MESH,
        )

    peers = [lax.rem(me + step, n) for step in range(1, n)]
    up, down = z + 1 < near, z >= 1

    for cut in range(CUTS):
        piece = x_ref.at[half * CUTS + cut]

        @pl.when(up)
        def _(piece=piece, cut=cut):
            chain_copy(piece, z, cut, 0, z + 1).start()

        @pl.when(down)
        def _(piece=piece, cut=cut):
            chain_copy(piece, z, cut, 1, z - 1).start()

    for part in range(2 * CUTS):
        core_copy(x_ref.at[part], z, part, k).start()
    for peer in peers:
        code_copy(peer, me).start()
    loads[3].wait()
    deep = grads.shape[0] // 2
    for head in range(n):
        cols = slice(head * DH, (head + 1) * DH)
        outbox[head] = jnp.concatenate([grads[:deep, cols], grads[deep:, cols]], axis=1)
    inbox[me] = outbox[me]
    for load in loads[:3] + loads[4:]:
        load.wait()
    factor = 1.0 / math.sqrt(DH)
    picked = [
        jnp.where(k == 0, weights[i, :, :DH], weights[i, :, DH:]) for i in range(3)
    ]
    for place, i in enumerate((0, 0, 1, 2)):
        weight[:, place * DH : (place + 1) * DH] = picked[i]

    def keep(origin):
        pair = pl.ds(2 * origin, 2)
        return pltpu.make_async_copy(x_all.at[pair], x_out.at[pair], keep_sem.at[origin])

    def project(origin):
        for part in range(2 * CUTS):
            core_copy(x_all.at[2 * origin + 1 - k, part], origin, part, 1 - k).wait_recv()
        keep(origin).start()
        for core in range(2):
            panel = 2 * origin + core
            x = x_all[panel].reshape(2 * deep, x_all.shape[3])
            made = jnp.dot(x, weight[...], preferred_element_type=jnp.float32)
            made = made.astype(jnp.bfloat16)
            queries = (made[:, :DH].astype(jnp.float32) * factor).astype(jnp.bfloat16)
            heads_ref[panel, :, :DH] = queries
            heads_ref[panel, :, 2 * DH :] = made[:, 2 * DH :]

    def through_row(origin, cut, there):
        @pl.when(there)
        def _():
            block = x_all.at[2 * origin + k, other * CUTS + cut]
            row_copy(block, origin, cut, other).wait_recv()
            core_copy(block, origin, other * CUTS + cut, k).start()

    def onto(origin, cut, there, onward, side, target):
        @pl.when(there)
        def _():
            block = x_all.at[2 * origin + k, half * CUTS + cut]
            chain_copy(block, origin, cut, side, z).wait_recv()

            @pl.when(onward)
            def _():
                chain_copy(block, origin, cut, side, target).start()

            row_copy(block, origin, cut, half).start()
            core_copy(block, origin, half * CUTS + cut, k).start()

    steps = []
    for d in range(1, near):
        for cut in range(CUTS):
            steps.append((z - d, cut, z - d >= 0, up, 0, z + 1))
            steps.append((z + d, cut, z + d < near, down, 1, z - 1))
    each = 2 * CUTS
    for step, (origin, cut, there, onward, side, target) in enumerate(steps):
        onto(origin, cut, there, onward, side, target)
        if step == min(2 * each, len(steps)) - 1:
            for peer in peers:
                grad_copy(peer, me).start()
        if step >= each:
            through_row(*steps[step - each][:3])
        if step == each - 1:
            project(z)
        if step >= 2 * each - 1 and (step + 1) % each == 0:
            for origin, _, there, _, _, _ in steps[step - 2 * each + 1 : step - 2 * each + 3]:
                pl.when(there)(functools.partial(project, origin))
    for origin, cut, there, _, _, _ in steps[-each:]:
        through_row(origin, cut, there)
    for peer in peers:
        grad_copy(peer, peer).wait_recv()
    for panel in range(n):
        heads_ref[panel, :deep, DH : 2 * DH] = inbox[panel, :, :DH]
        heads_ref[panel, deep:, DH : 2 * DH] = inbox[panel, :, DH:]
    for origin, _, there, _, _, _ in steps[-2:]:
        pl.when(there)(functools.partial(project, origin))
    for peer in peers:
        code_copy(peer, peer).wait_recv()
    for origin in range(near):
        keep(origin).wait()
    for peer in peers:
        code_copy(peer, me).wait_send()
        grad_copy(peer, me).wait_send()
    for cut in range(CUTS):
        piece = x_ref.at[half * CUTS + cut]

        @pl.when(up)
        def _(piece=piece, cut=cut):
            chain_copy(piece, z, cut, 0, z + 1).wait_send()

        @pl.when(down)
        def _(piece=piece, cut=cut):
            chain_copy(piece, z, cut, 1, z - 1).wait_send()

    for part in range(2 * CUTS):
        core_copy(x_ref.at[part], z, part, k).wait_send()
    for origin, cut, there, onward, side, target in steps:
        @pl.when(there)
        def _(origin=origin, cut=cut, onward=onward, side=side, target=target):
            block = x_all.at[2 * origin + k, half * CUTS + cut]

            @pl.when(onward)
            def _():
                chain_copy(block, origin, cut, side, target).wait_send()

            row_copy(block, origin, cut, half).wait_send()
            core_copy(block, origin, half * CUTS + cut, k).wait_send()
            core_copy(
                x_all.at[2 * origin + k, other * CUTS + cut], origin, other * CUTS + cut, k
            ).wait_send()


def spread(node_states, query_weight, key_weight, value_weight, output_grad, codes, n):
    rows, depth = node_states.shape
    width = 4 * DH
    near = n // 2
    vmem = pl.BlockSpec(memory_space=pltpu.VMEM)
    hbm = pl.BlockSpec(memory_space=pltpu.HBM)
    dma = pltpu.SemaphoreType.DMA
    return pl.pallas_call(
        functools.partial(spread_kernel, n),
        out_shape=(
            jax.ShapeDtypeStruct((n, rows, width), jnp.bfloat16),
            jax.ShapeDtypeStruct((n,) + codes.shape, jnp.int32),
            jax.ShapeDtypeStruct((n, 2 * CUTS, rows // (2 * CUTS), depth), jnp.bfloat16),
        ),
        in_specs=[hbm] * 5 + [vmem],
        out_specs=(vmem, vmem, hbm),
        scratch_shapes=[
            pltpu.VMEM((n, 2 * CUTS, rows // (2 * CUTS), depth), jnp.bfloat16),
            dma((near,)),
            pltpu.VMEM(output_grad.shape, jnp.bfloat16),
            pltpu.VMEM((3, depth, 2 * DH), jnp.bfloat16),
            pltpu.VMEM((depth, 4 * DH), jnp.bfloat16),
            pltpu.VMEM((n, rows // 2, 2 * DH), jnp.bfloat16),
            pltpu.VMEM((n, rows // 2, 2 * DH), jnp.bfloat16),
            dma((6,)), dma((n,)), dma((n,)), dma((n,)), dma((n,)),
            dma((2, near, CUTS)), dma((near, CUTS)), dma((near, 2 * CUTS)),
            dma((near, 2 * CUTS)), dma((near, CUTS)), dma((near, CUTS)),
        ],
        compiler_params=pltpu.CompilerParams(
            collective_id=0, has_side_effects=True, vmem_limit_bytes=54 << 20
        ),
        cost_estimate=pl.CostEstimate(
            flops=6 * rows * depth * n * DH, bytes_accessed=40 << 20, transcendentals=0
        ),
        name="spread_heads",
    )(
        node_states.reshape(2 * CUTS, rows // (2 * CUTS), depth), query_weight, key_weight, value_weight,
        output_grad, codes,
    )


def attend_kernel(
    n, blocks, codes_ref, heads_ref, out_ref, pairs_acc, scores_buf, grads_buf, kept, found, counts
):
    lanes = lax.broadcasted_iota(jnp.int32, (BLK, 2 * DH), 1)
    first = lanes < DH
    key_total = n * blocks
    nt = (((1,), (1,)), ((), ()))
    pairs_acc[...] = jnp.zeros_like(pairs_acc)

    def collect(panel):
        for q in range(blocks):
            counts[q] = 0
            for k in range(key_total):
                found[q, k] = 0
        total = codes_ref[panel, 2, 0]

        def one(slot, carry):
            q = codes_ref[panel, 0, slot]
            place = counts[q]
            found[q, place] = codes_ref[panel, 1, slot]
            counts[q] = place + 1
            return carry

        lax.fori_loop(0, total, one, 0)

    def work(panel, groups):
        width = GROUP * BLK
        stacks = []
        for q in range(blocks):
            both = heads_ref[panel, q * BLK : (q + 1) * BLK, : 2 * DH]
            zero = jnp.zeros_like(both)
            stacks.append(
                jnp.concatenate([jnp.where(first, both, zero), jnp.where(first, zero, both)], axis=0)
            )

        def table(q, g):
            parts = []
            for j in range(GROUP):
                k = found[q, g * GROUP + j]
                start = pl.multiple_of(lax.rem(k, blocks) * BLK, BLK)
                parts.append(heads_ref[lax.div(k, blocks), pl.ds(start, BLK), 2 * DH :])
            return jnp.concatenate(parts, axis=0)

        tops, totals, outs, deltas = [], [], [], []
        for q in range(blocks):
            top = jnp.full((BLK, BLK), LOWEST, jnp.float32)
            for g in range(groups):
                both = lax.dot_general(stacks[q], table(q, g), nt, preferred_element_type=jnp.float32)
                grads_buf[q, g] = both[BLK:]
                for j in range(GROUP):
                    tile = both[:BLK, j * BLK : (j + 1) * BLK]
                    live = g * GROUP + j < counts[q]
                    tile = jnp.where(live, tile, LOWEST)
                    scores_buf[q, g, :, j * BLK : (j + 1) * BLK] = tile
                    top = jnp.maximum(top, tile)
            tops.append(jnp.max(top, axis=1, keepdims=True))
        for q in range(blocks):
            total = jnp.zeros((BLK, BLK), jnp.float32)
            for g in range(groups):
                terms = jnp.exp(scores_buf[q, g] - tops[q])
                scores_buf[q, g] = terms
                for j in range(GROUP):
                    total = total + terms[:, j * BLK : (j + 1) * BLK]
            totals.append(1.0 / jnp.sum(total, axis=1, keepdims=True))
        for q in range(blocks):
            out = jnp.zeros((BLK, 2 * DH), jnp.float32)
            for g in range(groups):
                weights = (scores_buf[q, g] * totals[q]).astype(jnp.bfloat16)
                kept[q, g] = weights
                out = out + jnp.dot(weights, table(q, g), preferred_element_type=jnp.float32)
            outs.append(out)
            grad = stacks[q][BLK:].astype(jnp.float32)
            deltas.append(jnp.sum(grad * out, axis=1, keepdims=True))
        for q in range(blocks):
            rows_grad = jnp.zeros((BLK, 2 * DH), jnp.float32)
            turned = stacks[q].T
            for g in range(groups):
                weights = kept[q, g]
                score_grad = (
                    weights.astype(jnp.float32) * (grads_buf[q, g] - deltas[q])
                ).astype(jnp.bfloat16)
                rows_grad = rows_grad + jnp.dot(
                    score_grad, table(q, g), preferred_element_type=jnp.float32
                )
                pair = jnp.dot(
                    turned,
                    jnp.concatenate([score_grad, weights], axis=0),
                    preferred_element_type=jnp.float32,
                )
                for j in range(GROUP):
                    k = found[q, g * GROUP + j]
                    pairs_acc[k] = pairs_acc[k] + pair[:, j * BLK : (j + 1) * BLK]
            factor = 1.0 / math.sqrt(DH)
            out_ref[panel, q * BLK : (q + 1) * BLK, : 2 * DH] = jnp.where(
                first, rows_grad * factor, outs[q]
            ).astype(jnp.bfloat16)

    def one_panel(panel, carry):
        collect(panel)
        most = counts[0]
        for q in range(1, blocks):
            most = jnp.maximum(most, counts[q])
        groups = lax.div(most + (GROUP - 1), GROUP)
        for size in range(1, key_total // GROUP + 1):
            pl.when(groups == size)(functools.partial(work, panel, size))
        return carry

    lax.fori_loop(0, n, one_panel, 0)
    for k in range(key_total):
        row = (k % blocks) * BLK
        out_ref[k // blocks, row : row + BLK, 2 * DH :] = pairs_acc[k].T.astype(jnp.bfloat16)


def attend(heads, codes, n, blocks):
    key_total = n * blocks
    groups = key_total // GROUP
    tiles = key_total * key_total
    return pl.pallas_call(
        functools.partial(attend_kernel, n, blocks),
        out_shape=jax.ShapeDtypeStruct(heads.shape, jnp.bfloat16),
        in_specs=[
            pl.BlockSpec(memory_space=pltpu.SMEM),
            pl.BlockSpec(memory_space=pltpu.VMEM),
        ],
        out_specs=pl.BlockSpec(memory_space=pltpu.VMEM),
        scratch_shapes=[
            pltpu.VMEM((key_total, 2 * DH, BLK), jnp.float32),
            pltpu.VMEM((blocks, groups, BLK, GROUP * BLK), jnp.float32),
            pltpu.VMEM((blocks, groups, BLK, GROUP * BLK), jnp.float32),
            pltpu.VMEM((blocks, groups, BLK, GROUP * BLK), jnp.bfloat16),
            pltpu.SMEM((blocks, key_total), jnp.int32),
            pltpu.SMEM((blocks,), jnp.int32),
        ],
        compiler_params=pltpu.CompilerParams(vmem_limit_bytes=16 << 20),
        cost_estimate=pl.CostEstimate(
            flops=tiles * 24 * BLK * BLK * DH, bytes_accessed=80 << 20,
            transcendentals=tiles * BLK * BLK,
        ),
        name="attend_heads",
    )(codes, heads)


def collect_kernel(
    n, n_row, res_ref, x_ref, wq_ref, wk_ref, wv_ref,
    att_ref, terms_in, part_in,
    inbox, terms_out, part_out,
    send_sem, recv_sem, term_send, term_recv, row_send, row_recv,
):
    me = lax.axis_index("col")
    my_row = lax.axis_index("row")
    meet([("col", n), ("row", n_row)])
    peers = [lax.rem(me + step, n) for step in range(1, n)]
    row_peers = [lax.rem(my_row + step, n_row) for step in range(1, n_row)]
    cols = part_out.shape[2]

    def res_copy(peer, slot):
        return pltpu.make_async_remote_copy(
            src_ref=res_ref.at[peer], dst_ref=inbox.at[slot], send_sem=send_sem.at[peer],
            recv_sem=recv_sem.at[slot], device_id={"col": peer}, device_id_type=MESH,
        )

    def term_copy(peer, slot):
        return pltpu.make_async_remote_copy(
            src_ref=terms_out.at[peer], dst_ref=terms_in.at[slot], send_sem=term_send.at[peer],
            recv_sem=term_recv.at[slot], device_id={"col": peer}, device_id_type=MESH,
        )

    def row_copy(peer, slot):
        return pltpu.make_async_remote_copy(
            src_ref=part_out.at[peer], dst_ref=part_in.at[slot], send_sem=row_send.at[peer],
            recv_sem=row_recv.at[slot], device_id={"row": peer}, device_id_type=MESH,
        )

    for peer in peers:
        res_copy(peer, me).start()
    inbox[me] = res_ref[me]
    rows = res_ref.shape[1]
    depth = x_ref.shape[3]
    chunk = depth // n
    turned = res_ref[...].reshape(n * rows, 4 * DH).T
    for peer in range(n):
        term = jnp.dot(
            turned,
            x_ref[:, :, :, peer * chunk : (peer + 1) * chunk].reshape(n * rows, chunk),
            preferred_element_type=jnp.float32,
        ).astype(jnp.bfloat16)
        terms_out[peer, :DH] = term[:DH]
        terms_out[peer, DH:] = term[2 * DH :]
    terms_in[me] = terms_out[me]
    for peer in peers:
        res_copy(peer, peer).wait_recv()
    for peer in peers:
        term_copy(peer, me).start()

    def piece(which):
        return jnp.concatenate(
            [inbox[h, :, which * DH : (which + 1) * DH] for h in range(n)], axis=1
        )

    nt = (((1,), (1,)), ((), ()))
    grads = [piece(0), piece(2), piece(3)]
    weights = [wq_ref, wk_ref, wv_ref]
    for r in range(n_row):
        span = slice(r * cols, (r + 1) * cols)
        part = jnp.zeros((rows, cols), jnp.float32)
        for grad, weight in zip(grads, weights):
            part = part + lax.dot_general(
                grad, weight[span, :], nt, preferred_element_type=jnp.float32
            )
        part_out[r] = part.astype(jnp.bfloat16)
    for peer in row_peers:
        row_copy(peer, my_row).start()
    att_ref[...] = piece(1)
    for peer in peers:
        term_copy(peer, peer).wait_recv()
    part_in[my_row] = part_out[my_row]
    for peer in row_peers:
        row_copy(peer, peer).wait_recv()
    for peer in peers:
        res_copy(peer, me).wait_send()
        term_copy(peer, me).wait_send()
    for peer in row_peers:
        row_copy(peer, my_row).wait_send()


def finish_kernel(
    n, n_row, att_in, terms, parts, att_ref, node_ref, qg_ref, kg_ref, vg_ref,
    node_buf, grad_buf, sem,
):
    copies = [pltpu.make_async_copy(att_in, att_ref, sem.at[0])]
    copies[0].start()
    total = parts[0].astype(jnp.float32)
    for r in range(1, n_row):
        total = total + parts[r].astype(jnp.float32)
    node_buf[...] = total
    copies.append(pltpu.make_async_copy(node_buf, node_ref, sem.at[1]))
    copies[1].start()
    for which, ref in enumerate((qg_ref, kg_ref, vg_ref)):
        for h in range(0, n, 2):
            pair = jnp.concatenate(
                [
                    terms[h, which * DH : (which + 1) * DH],
                    terms[h + 1, which * DH : (which + 1) * DH],
                ],
                axis=0,
            )
            grad_buf[which, :, h * DH : (h + 2) * DH] = pair.astype(jnp.float32).T
        copies.append(pltpu.make_async_copy(grad_buf.at[which], ref, sem.at[2 + which]))
        copies[-1].start()
    for copy in copies:
        copy.wait()


def collect_grads(res, x_all, query_weight, key_weight, value_weight, n, n_row):
    rows = res.shape[1]
    depth = x_all.shape[3]
    cols = depth // n_row
    chunk = depth // n
    head_cols = n * DH
    vmem = pl.BlockSpec(memory_space=pltpu.VMEM)
    hbm = pl.BlockSpec(memory_space=pltpu.HBM)
    dma = pltpu.SemaphoreType.DMA
    att, terms, parts = pl.pallas_call(
        functools.partial(collect_kernel, n, n_row),
        out_shape=(
            jax.ShapeDtypeStruct((rows, head_cols), jnp.bfloat16),
            jax.ShapeDtypeStruct((n, 3 * DH, chunk), jnp.bfloat16),
            jax.ShapeDtypeStruct((n_row, rows, cols), jnp.bfloat16),
        ),
        in_specs=[vmem] * 5,
        out_specs=(vmem,) * 3,
        scratch_shapes=[
            pltpu.VMEM(res.shape, jnp.bfloat16),
            pltpu.VMEM((n, 3 * DH, chunk), jnp.bfloat16),
            pltpu.VMEM((n_row, rows, cols), jnp.bfloat16),
            dma((n,)), dma((n,)), dma((n,)), dma((n,)), dma((n_row,)), dma((n_row,)),
        ],
        compiler_params=pltpu.CompilerParams(
            collective_id=1, has_side_effects=True, vmem_limit_bytes=20 << 20
        ),
        name="collect_grads",
    )(res, x_all, query_weight, key_weight, value_weight)
    return pl.pallas_call(
        functools.partial(finish_kernel, n, n_row),
        out_shape=(
            jax.ShapeDtypeStruct((rows, head_cols), jnp.bfloat16),
            jax.ShapeDtypeStruct((rows, cols), jnp.float32),
            jax.ShapeDtypeStruct((chunk, head_cols), jnp.float32),
            jax.ShapeDtypeStruct((chunk, head_cols), jnp.float32),
            jax.ShapeDtypeStruct((chunk, head_cols), jnp.float32),
        ),
        in_specs=[vmem] * 3,
        out_specs=(hbm,) * 5,
        scratch_shapes=[
            pltpu.VMEM((rows, cols), jnp.float32),
            pltpu.VMEM((3, chunk, head_cols), jnp.float32),
            dma((5,)),
        ],
        compiler_params=pltpu.CompilerParams(vmem_limit_bytes=16 << 20),
        name="finish",
    )(att, terms, parts)


def per_device_heads(
    n, n_row, node_states, query_weight, key_weight, value_weight, output_grad, pair_list, pair_count
):
    blocks = node_states.shape[0] // BLK
    slots = pair_list.shape[1]
    listed = jnp.pad(pair_list[0].T, ((0, 0), (0, BLK - slots)))
    total = jnp.broadcast_to(pair_count[0], (6, BLK))
    codes = jnp.concatenate([listed, total], axis=0)
    heads, codes_all, x_all = spread(
        node_states, query_weight, key_weight, value_weight, output_grad, codes, n
    )
    res = attend(heads, codes_all, n, blocks)
    return collect_grads(res, x_all, query_weight, key_weight, value_weight, n, n_row)


def per_device(mesh, *arrays):
    n, n_row = mesh.shape["col"], mesh.shape["row"]
    node_states, query_weight, pair_list = arrays[0], arrays[1], arrays[5]
    blocks = node_states.shape[0] // BLK
    one_head_each = query_weight.shape[1] == n * DH and n % 2 == 0 and n_row == 2
    tiled = (n * blocks) % GROUP == 0 and pair_list.shape[1] <= BLK
    lanes = node_states.shape[1] % (n * BLK) == 0 and node_states.shape[1] % (n_row * BLK) == 0
    if one_head_each and tiled and lanes:
        return per_device_heads(n, n_row, *arrays)
    return per_device_slots(*arrays)


def solution(mesh):
    return jax.shard_map(
        functools.partial(per_device, mesh),
        mesh=mesh,
        in_specs=(
            P(("groups", "col"), None),
            P(None, "row"),
            P(None, "row"),
            P(None, "row"),
            P(("groups", "col"), "row"),
            P(("groups", "col"), None, None),
            P(("groups", "col")),
        ),
        out_specs=(
            P(("groups", "col"), "row"),
            P(("groups", "col"), "row"),
            P(("groups", "col"), "row"),
            P(("groups", "col"), "row"),
            P(("groups", "col"), "row"),
        ),
        check_vma=False,
    )
```

```python
import functools
import math

import jax
import jax.numpy as jnp
from jax import lax
from jax.experimental import pallas as pl
from jax.experimental.pallas import tpu as pltpu
from jax.sharding import PartitionSpec as P

DH = 64
BLK = 128


LOWEST = -1e30
EXACT = lax.Precision.HIGHEST


def slot_batch(pair_rows, pair_total, turn_index, width, blocks):
    start = turn_index * width
    query_block = pair_rows[:, 0]
    key_block = pair_rows[:, 1]
    slot_live = start + jnp.arange(width, dtype=jnp.int32) < pair_total
    owners = jnp.logical_and(
        query_block[:, None] == jnp.arange(blocks, dtype=jnp.int32)[None, :], slot_live[:, None]
    )
    return (query_block, key_block, slot_live, owners)


def batch_tiles(query_tiles, table_tiles, query_block, key_block, head_cols, factor):
    head_count = head_cols // DH
    width = query_block.shape[0]
    query_pick = jnp.take(query_tiles, query_block, axis=0)
    table_pick = jnp.take(table_tiles, key_block, axis=0)
    key_pick = table_pick[:, :, :head_cols].reshape(width, BLK, head_count, DH)
    value_pick = table_pick[:, :, head_cols:].reshape(width, BLK, head_count, DH)
    scores = (
        jnp.einsum("sihd,sjhd->shij", query_pick, key_pick, preferred_element_type=jnp.float32)
        * factor
    )
    return (query_pick, key_pick, value_pick, scores)


def batch_weights(scores, row_top, totals, query_block, slot_live):
    top_pick = jnp.take(row_top, query_block, axis=0)
    total_pick = jnp.take(totals, query_block, axis=0)
    weights = jnp.exp(scores - top_pick[..., None]) / total_pick[..., None]
    return jnp.where(slot_live[:, None, None, None], weights, 0.0).astype(jnp.bfloat16)


def per_device_slots(
    node_states, query_weight, key_weight, value_weight, output_grad, pair_list, pair_count
):
    head_cols = query_weight.shape[1]
    head_count = head_cols // DH
    panel_rows = node_states.shape[0]
    blocks = panel_rows // BLK
    factor = 1.0 / math.sqrt(DH)
    pair_rows = pair_list[0]
    pair_total = pair_count[0]
    width = math.gcd(pair_rows.shape[0], 32)
    turns = (pair_total + width - 1) // width
    queries = jnp.dot(node_states, query_weight, preferred_element_type=jnp.float32).astype(
        jnp.bfloat16
    )
    keys_here = jnp.dot(node_states, key_weight, preferred_element_type=jnp.float32).astype(
        jnp.bfloat16
    )
    values_here = jnp.dot(node_states, value_weight, preferred_element_type=jnp.float32).astype(
        jnp.bfloat16
    )
    local_table = jnp.concatenate([keys_here, values_here], axis=1)
    key_table = lax.all_gather(local_table, "col", axis=0, tiled=True)
    key_blocks_all = key_table.shape[0] // BLK
    query_tiles = queries.reshape(blocks, BLK, head_count, DH)
    table_tiles = key_table.reshape(key_blocks_all, BLK, 2 * head_cols)

    def stats_turn(turn_index, state_pair):
        row_top, totals = state_pair
        query_block, key_block, slot_live, owners = slot_batch(
            pair_rows, pair_total, turn_index, width, blocks
        )
        scores = batch_tiles(query_tiles, table_tiles, query_block, key_block, head_cols, factor)[3]
        pair_top = jnp.max(scores, axis=3)
        block_top = jnp.max(jnp.where(owners[:, :, None, None], pair_top[:, None], LOWEST), axis=0)
        new_top = jnp.maximum(row_top, block_top)
        top_pick = jnp.take(new_top, query_block, axis=0)
        exp_terms = jnp.where(
            slot_live[:, None, None, None], jnp.exp(scores - top_pick[..., None]), 0.0
        )
        added = jnp.einsum(
            "sn,shi->nhi", owners.astype(jnp.float32), jnp.sum(exp_terms, axis=3), precision=EXACT
        )
        totals = totals * jnp.exp(row_top - new_top) + added
        return (new_top, totals)

    start_top = jnp.full((blocks, head_count, BLK), LOWEST, jnp.float32)
    start_total = jnp.zeros((blocks, head_count, BLK), jnp.float32)
    row_top, totals = lax.fori_loop(0, turns, stats_turn, (start_top, start_total))

    def attend_turn(turn_index, output):
        query_block, key_block, slot_live, owners = slot_batch(
            pair_rows, pair_total, turn_index, width, blocks
        )
        query_pick, key_pick, value_pick, scores = batch_tiles(
            query_tiles, table_tiles, query_block, key_block, head_cols, factor
        )
        weights = batch_weights(scores, row_top, totals, query_block, slot_live)
        update = jnp.einsum(
            "shij,sjhd->sihd", weights, value_pick, preferred_element_type=jnp.float32
        )
        return output + jnp.einsum(
            "sn,sihd->nihd", owners.astype(jnp.float32), update, precision=EXACT
        )

    output = lax.fori_loop(
        0, turns, attend_turn, jnp.zeros((blocks, BLK, head_count, DH), jnp.float32)
    )
    attended = output.reshape(panel_rows, head_cols).astype(jnp.bfloat16)
    grad_tiles = output_grad.reshape(blocks, BLK, head_count, DH)
    deltas = jnp.sum(grad_tiles.astype(jnp.float32) * output, axis=3)
    back_table = lax.all_gather(local_table, "col", axis=0, tiled=True)
    back_tiles = back_table.reshape(key_blocks_all, BLK, 2 * head_cols)

    def backward_turn(turn_index, state_pair):
        grad_rows, key_grads = state_pair
        query_block, key_block, slot_live, owners = slot_batch(
            pair_rows, pair_total, turn_index, width, blocks
        )
        query_pick, key_pick, value_pick, scores = batch_tiles(
            query_tiles, back_tiles, query_block, key_block, head_cols, factor
        )
        weights = batch_weights(scores, row_top, totals, query_block, slot_live)
        grad_pick = jnp.take(grad_tiles, query_block, axis=0)
        value_part = jnp.einsum(
            "shij,sihd->sjhd", weights, grad_pick, preferred_element_type=jnp.float32
        )
        prob_grad = jnp.einsum(
            "sihd,sjhd->shij", grad_pick, value_pick, preferred_element_type=jnp.float32
        )
        delta_pick = jnp.transpose(jnp.take(deltas, query_block, axis=0), (0, 2, 1))
        score_grad = (weights.astype(jnp.float32) * (prob_grad - delta_pick[..., None])).astype(
            jnp.bfloat16
        )
        query_part = (
            jnp.einsum("shij,sjhd->sihd", score_grad, key_pick, preferred_element_type=jnp.float32)
            * factor
        )
        key_part = (
            jnp.einsum(
                "shij,sihd->sjhd", score_grad, query_pick, preferred_element_type=jnp.float32
            )
            * factor
        )
        grad_rows = grad_rows + jnp.einsum(
            "sn,sihd->nihd", owners.astype(jnp.float32), query_part, precision=EXACT
        )
        rows_update = jnp.concatenate(
            [key_part.reshape(width, BLK, head_cols), value_part.reshape(width, BLK, head_cols)],
            axis=2,
        )
        key_grads = key_grads + jax.ops.segment_sum(
            rows_update, key_block, num_segments=key_blocks_all
        )
        return (grad_rows, key_grads)

    start_rows = jnp.zeros((blocks, BLK, head_count, DH), jnp.float32)
    start_keys = jnp.zeros((key_blocks_all, BLK, 2 * head_cols), jnp.float32)
    grad_rows, key_grads = lax.fori_loop(0, turns, backward_turn, (start_rows, start_keys))
    key_grads = key_grads.reshape(key_blocks_all * BLK, 2 * head_cols)
    pair_grads = lax.psum_scatter(
        key_grads.astype(jnp.bfloat16), "col", scatter_dimension=0, tiled=True
    ).astype(jnp.float32)
    query_rows_grad = grad_rows.reshape(panel_rows, head_cols).astype(jnp.bfloat16)
    key_rows_grad = pair_grads[:, :head_cols].astype(jnp.bfloat16)
    value_rows_grad = pair_grads[:, head_cols:].astype(jnp.bfloat16)
    contract = (((1,), (1,)), ((), ()))
    partial_sum = lax.dot_general(
        query_rows_grad, query_weight, contract, preferred_element_type=jnp.float32
    )
    partial_sum = partial_sum + lax.dot_general(
        key_rows_grad, key_weight, contract, preferred_element_type=jnp.float32
    )
    partial_sum = partial_sum + lax.dot_general(
        value_rows_grad, value_weight, contract, preferred_element_type=jnp.float32
    )
    node_grad = lax.psum_scatter(
        partial_sum.astype(jnp.bfloat16), "row", scatter_dimension=1, tiled=True
    ).astype(jnp.float32)
    over_nodes = (((0,), (0,)), ((), ()))
    query_term = lax.dot_general(
        node_states, query_rows_grad, over_nodes, preferred_element_type=jnp.float32
    )
    key_term = lax.dot_general(
        node_states, key_rows_grad, over_nodes, preferred_element_type=jnp.float32
    )
    value_term = lax.dot_general(
        node_states, value_rows_grad, over_nodes, preferred_element_type=jnp.float32
    )
    query_grad, key_grad, value_grad = (
        lax.psum_scatter(
            query_term.astype(jnp.bfloat16), "col", scatter_dimension=0, tiled=True
        ).astype(jnp.float32),
        lax.psum_scatter(
            key_term.astype(jnp.bfloat16), "col", scatter_dimension=0, tiled=True
        ).astype(jnp.float32),
        lax.psum_scatter(
            value_term.astype(jnp.bfloat16), "col", scatter_dimension=0, tiled=True
        ).astype(jnp.float32),
    )
    return (attended, node_grad, query_grad, key_grad, value_grad)


MESH = pl.DeviceIdType.MESH
GROUP = 2
CUTS = 4


def meet(axes):
    barrier = pltpu.get_barrier_semaphore()
    total = 0
    for axis, count in axes:
        me = lax.axis_index(axis)
        for step in range(1, count):
            peer = lax.rem(me + step, count)
            pl.semaphore_signal(barrier, inc=1, device_id={axis: peer}, device_id_type=MESH)
            total += 1
    pl.semaphore_wait(barrier, total)


def spread_kernel(
    n, x_ref, wq_ref, wk_ref, wv_ref, grad_ref, code_ref, heads_ref, codes_ref, x_out,
    x_all, keep_sem, grads, weights, weight, outbox, inbox, load_sem, grad_send, grad_recv, code_send, code_recv,
    chain_send, chain_recv, core_send, core_recv, row_send, row_recv,
):
    me = lax.axis_index("col")
    half = lax.axis_index("row")
    other = 1 - half
    near = n // 2
    z = lax.div(me, 2)
    k = lax.rem(me, 2)
    twin = 2 * z + 1 - k

    loads = [
        pltpu.make_async_copy(
            ref.at[:, pl.ds(pl.multiple_of(z * 2 * DH, 2 * DH), 2 * DH)],
            weights.at[i],
            load_sem.at[i],
        )
        for i, ref in enumerate((wq_ref, wk_ref, wv_ref))
    ]
    loads.append(pltpu.make_async_copy(grad_ref, grads, load_sem.at[3]))
    loads.append(pltpu.make_async_copy(x_ref, x_all.at[me], load_sem.at[4]))
    loads.append(pltpu.make_async_copy(code_ref, codes_ref.at[me], load_sem.at[5]))
    for load in loads:
        load.start()
    meet([("col", n), ("row", 2)])

    def code_copy(peer, slot):
        return pltpu.make_async_remote_copy(
            src_ref=code_ref, dst_ref=codes_ref.at[slot], send_sem=code_send.at[peer],
            recv_sem=code_recv.at[slot], device_id={"col": peer}, device_id_type=MESH,
        )

    def grad_copy(peer, slot):
        return pltpu.make_async_remote_copy(
            src_ref=outbox.at[peer], dst_ref=inbox.at[slot], send_sem=grad_send.at[peer],
            recv_sem=grad_recv.at[slot], device_id={"col": peer}, device_id_type=MESH,
        )

    def chain_copy(src, origin, cut, side, target):
        return pltpu.make_async_remote_copy(
            src_ref=src, dst_ref=x_all.at[2 * origin + k, half * CUTS + cut],
            send_sem=chain_send.at[side, origin, cut], recv_sem=chain_recv.at[origin, cut],
            device_id={"col": 2 * target + k}, device_id_type=MESH,
        )

    def core_copy(src, origin, part, core):
        return pltpu.make_async_remote_copy(
            src_ref=src, dst_ref=x_all.at[2 * origin + core, part],
            send_sem=core_send.at[origin, part], recv_sem=core_recv.at[origin, part],
            device_id={"col": twin}, device_id_type=MESH,
        )

    def row_copy(src, origin, cut, part):
        return pltpu.make_async_remote_copy(
            src_ref=src, dst_ref=x_all.at[2 * origin + k, part * CUTS + cut],
            send_sem=row_send.at[origin, cut], recv_sem=row_recv.at[origin, cut],
            device_id={"row": other}, device_id_type=MESH,
        )

    peers = [lax.rem(me + step, n) for step in range(1, n)]
    up, down = z + 1 < near, z >= 1

    for cut in range(CUTS):
        piece = x_ref.at[half * CUTS + cut]

        @pl.when(up)
        def _(piece=piece, cut=cut):
            chain_copy(piece, z, cut, 0, z + 1).start()

        @pl.when(down)
        def _(piece=piece, cut=cut):
            chain_copy(piece, z, cut, 1, z - 1).start()

    for part in range(2 * CUTS):
        core_copy(x_ref.at[part], z, part, k).start()
    for peer in peers:
        code_copy(peer, me).start()
    loads[3].wait()
    deep = grads.shape[0] // 2
    for head in range(n):
        cols = slice(head * DH, (head + 1) * DH)
        outbox[head] = jnp.concatenate([grads[:deep, cols], grads[deep:, cols]], axis=1)
    inbox[me] = outbox[me]
    for load in loads[:3] + loads[4:]:
        load.wait()
    factor = 1.0 / math.sqrt(DH)
    picked = [
        jnp.where(k == 0, weights[i, :, :DH], weights[i, :, DH:]) for i in range(3)
    ]
    for place, i in enumerate((0, 0, 1, 2)):
        weight[:, place * DH : (place + 1) * DH] = picked[i]

    def keep(origin):
        pair = pl.ds(2 * origin, 2)
        return pltpu.make_async_copy(x_all.at[pair], x_out.at[pair], keep_sem.at[origin])

    def project(origin):
        for part in range(2 * CUTS):
            core_copy(x_all.at[2 * origin + 1 - k, part], origin, part, 1 - k).wait_recv()
        keep(origin).start()
        for core in range(2):
            panel = 2 * origin + core
            x = x_all[panel].reshape(2 * deep, x_all.shape[3])
            made = jnp.dot(x, weight[...], preferred_element_type=jnp.float32)
            made = made.astype(jnp.bfloat16)
            queries = (made[:, :DH].astype(jnp.float32) * factor).astype(jnp.bfloat16)
            heads_ref[panel, :, :DH] = queries
            heads_ref[panel, :, 2 * DH :] = made[:, 2 * DH :]

    def through_row(origin, cut, there):
        @pl.when(there)
        def _():
            block = x_all.at[2 * origin + k, other * CUTS + cut]
            row_copy(block, origin, cut, other).wait_recv()
            core_copy(block, origin, other * CUTS + cut, k).start()

    def onto(origin, cut, there, onward, side, target):
        @pl.when(there)
        def _():
            block = x_all.at[2 * origin + k, half * CUTS + cut]
            chain_copy(block, origin, cut, side, z).wait_recv()

            @pl.when(onward)
            def _():
                chain_copy(block, origin, cut, side, target).start()

            row_copy(block, origin, cut, half).start()
            core_copy(block, origin, half * CUTS + cut, k).start()

    steps = []
    for d in range(1, near):
        for cut in range(CUTS):
            steps.append((z - d, cut, z - d >= 0, up, 0, z + 1))
            steps.append((z + d, cut, z + d < near, down, 1, z - 1))
    each = 2 * CUTS
    for step, (origin, cut, there, onward, side, target) in enumerate(steps):
        onto(origin, cut, there, onward, side, target)
        if step == min(2 * each, len(steps)) - 1:
            for peer in peers:
                grad_copy(peer, me).start()
        if step >= each:
            through_row(*steps[step - each][:3])
        if step == each - 1:
            project(z)
        if step >= 2 * each - 1 and (step + 1) % each == 0:
            for origin, _, there, _, _, _ in steps[step - 2 * each + 1 : step - 2 * each + 3]:
                pl.when(there)(functools.partial(project, origin))
    for origin, cut, there, _, _, _ in steps[-each:]:
        through_row(origin, cut, there)
    for peer in peers:
        grad_copy(peer, peer).wait_recv()
    for panel in range(n):
        heads_ref[panel, :deep, DH : 2 * DH] = inbox[panel, :, :DH]
        heads_ref[panel, deep:, DH : 2 * DH] = inbox[panel, :, DH:]
    for origin, _, there, _, _, _ in steps[-2:]:
        pl.when(there)(functools.partial(project, origin))
    for peer in peers:
        code_copy(peer, peer).wait_recv()
    for origin in range(near):
        keep(origin).wait()
    for peer in peers:
        code_copy(peer, me).wait_send()
        grad_copy(peer, me).wait_send()
    for cut in range(CUTS):
        piece = x_ref.at[half * CUTS + cut]

        @pl.when(up)
        def _(piece=piece, cut=cut):
            chain_copy(piece, z, cut, 0, z + 1).wait_send()

        @pl.when(down)
        def _(piece=piece, cut=cut):
            chain_copy(piece, z, cut, 1, z - 1).wait_send()

    for part in range(2 * CUTS):
        core_copy(x_ref.at[part], z, part, k).wait_send()
    for origin, cut, there, onward, side, target in steps:
        @pl.when(there)
        def _(origin=origin, cut=cut, onward=onward, side=side, target=target):
            block = x_all.at[2 * origin + k, half * CUTS + cut]

            @pl.when(onward)
            def _():
                chain_copy(block, origin, cut, side, target).wait_send()

            row_copy(block, origin, cut, half).wait_send()
            core_copy(block, origin, half * CUTS + cut, k).wait_send()
            core_copy(
                x_all.at[2 * origin + k, other * CUTS + cut], origin, other * CUTS + cut, k
            ).wait_send()


def spread(node_states, query_weight, key_weight, value_weight, output_grad, codes, n):
    rows, depth = node_states.shape
    width = 4 * DH
    near = n // 2
    vmem = pl.BlockSpec(memory_space=pltpu.VMEM)
    hbm = pl.BlockSpec(memory_space=pltpu.HBM)
    dma = pltpu.SemaphoreType.DMA
    return pl.pallas_call(
        functools.partial(spread_kernel, n),
        out_shape=(
            jax.ShapeDtypeStruct((n, rows, width), jnp.bfloat16),
            jax.ShapeDtypeStruct((n,) + codes.shape, jnp.int32),
            jax.ShapeDtypeStruct((n, 2 * CUTS, rows // (2 * CUTS), depth), jnp.bfloat16),
        ),
        in_specs=[hbm] * 5 + [vmem],
        out_specs=(vmem, vmem, hbm),
        scratch_shapes=[
            pltpu.VMEM((n, 2 * CUTS, rows // (2 * CUTS), depth), jnp.bfloat16),
            dma((near,)),
            pltpu.VMEM(output_grad.shape, jnp.bfloat16),
            pltpu.VMEM((3, depth, 2 * DH), jnp.bfloat16),
            pltpu.VMEM((depth, 4 * DH), jnp.bfloat16),
            pltpu.VMEM((n, rows // 2, 2 * DH), jnp.bfloat16),
            pltpu.VMEM((n, rows // 2, 2 * DH), jnp.bfloat16),
            dma((6,)), dma((n,)), dma((n,)), dma((n,)), dma((n,)),
            dma((2, near, CUTS)), dma((near, CUTS)), dma((near, 2 * CUTS)),
            dma((near, 2 * CUTS)), dma((near, CUTS)), dma((near, CUTS)),
        ],
        compiler_params=pltpu.CompilerParams(
            collective_id=0, has_side_effects=True, vmem_limit_bytes=54 << 20
        ),
        cost_estimate=pl.CostEstimate(
            flops=6 * rows * depth * n * DH, bytes_accessed=40 << 20, transcendentals=0
        ),
        name="spread_heads",
    )(
        node_states.reshape(2 * CUTS, rows // (2 * CUTS), depth), query_weight, key_weight, value_weight,
        output_grad, codes,
    )


def attend_kernel(
    n, blocks, codes_ref, heads_ref, out_ref, pairs_acc, scores_buf, grads_buf, kept, found, counts
):
    lanes = lax.broadcasted_iota(jnp.int32, (BLK, 2 * DH), 1)
    first = lanes < DH
    key_total = n * blocks
    nt = (((1,), (1,)), ((), ()))
    pairs_acc[...] = jnp.zeros_like(pairs_acc)

    def collect(panel):
        for q in range(blocks):
            counts[q] = 0
            for k in range(key_total):
                found[q, k] = 0
        total = codes_ref[panel, 2, 0]

        def one(slot, carry):
            q = codes_ref[panel, 0, slot]
            place = counts[q]
            found[q, place] = codes_ref[panel, 1, slot]
            counts[q] = place + 1
            return carry

        lax.fori_loop(0, total, one, 0)

    def work(panel, groups):
        width = GROUP * BLK
        stacks = []
        for q in range(blocks):
            both = heads_ref[panel, q * BLK : (q + 1) * BLK, : 2 * DH]
            zero = jnp.zeros_like(both)
            stacks.append(
                jnp.concatenate([jnp.where(first, both, zero), jnp.where(first, zero, both)], axis=0)
            )

        def table(q, g):
            parts = []
            for j in range(GROUP):
                k = found[q, g * GROUP + j]
                start = pl.multiple_of(lax.rem(k, blocks) * BLK, BLK)
                parts.append(heads_ref[lax.div(k, blocks), pl.ds(start, BLK), 2 * DH :])
            return jnp.concatenate(parts, axis=0)

        tops, totals, outs, deltas = [], [], [], []
        for q in range(blocks):
            top = jnp.full((BLK, BLK), LOWEST, jnp.float32)
            for g in range(groups):
                both = lax.dot_general(stacks[q], table(q, g), nt, preferred_element_type=jnp.float32)
                grads_buf[q, g] = both[BLK:]
                for j in range(GROUP):
                    tile = both[:BLK, j * BLK : (j + 1) * BLK]
                    live = g * GROUP + j < counts[q]
                    tile = jnp.where(live, tile, LOWEST)
                    scores_buf[q, g, :, j * BLK : (j + 1) * BLK] = tile
                    top = jnp.maximum(top, tile)
            tops.append(jnp.max(top, axis=1, keepdims=True))
        for q in range(blocks):
            total = jnp.zeros((BLK, BLK), jnp.float32)
            for g in range(groups):
                terms = jnp.exp(scores_buf[q, g] - tops[q])
                scores_buf[q, g] = terms
                for j in range(GROUP):
                    total = total + terms[:, j * BLK : (j + 1) * BLK]
            totals.append(1.0 / jnp.sum(total, axis=1, keepdims=True))
        for q in range(blocks):
            out = jnp.zeros((BLK, 2 * DH), jnp.float32)
            for g in range(groups):
                weights = (scores_buf[q, g] * totals[q]).astype(jnp.bfloat16)
                kept[q, g] = weights
                out = out + jnp.dot(weights, table(q, g), preferred_element_type=jnp.float32)
            outs.append(out)
            grad = stacks[q][BLK:].astype(jnp.float32)
            deltas.append(jnp.sum(grad * out, axis=1, keepdims=True))
        for q in range(blocks):
            rows_grad = jnp.zeros((BLK, 2 * DH), jnp.float32)
            turned = stacks[q].T
            for g in range(groups):
                weights = kept[q, g]
                score_grad = (
                    weights.astype(jnp.float32) * (grads_buf[q, g] - deltas[q])
                ).astype(jnp.bfloat16)
                rows_grad = rows_grad + jnp.dot(
                    score_grad, table(q, g), preferred_element_type=jnp.float32
                )
                pair = jnp.dot(
                    turned,
                    jnp.concatenate([score_grad, weights], axis=0),
                    preferred_element_type=jnp.float32,
                )
                for j in range(GROUP):
                    k = found[q, g * GROUP + j]
                    pairs_acc[k] = pairs_acc[k] + pair[:, j * BLK : (j + 1) * BLK]
            factor = 1.0 / math.sqrt(DH)
            out_ref[panel, q * BLK : (q + 1) * BLK, : 2 * DH] = jnp.where(
                first, rows_grad * factor, outs[q]
            ).astype(jnp.bfloat16)

    def one_panel(panel, carry):
        collect(panel)
        most = counts[0]
        for q in range(1, blocks):
            most = jnp.maximum(most, counts[q])
        groups = lax.div(most + (GROUP - 1), GROUP)
        for size in range(1, key_total // GROUP + 1):
            pl.when(groups == size)(functools.partial(work, panel, size))
        return carry

    lax.fori_loop(0, n, one_panel, 0)
    for k in range(key_total):
        row = (k % blocks) * BLK
        out_ref[k // blocks, row : row + BLK, 2 * DH :] = pairs_acc[k].T.astype(jnp.bfloat16)


def attend(heads, codes, n, blocks):
    key_total = n * blocks
    groups = key_total // GROUP
    tiles = key_total * key_total
    return pl.pallas_call(
        functools.partial(attend_kernel, n, blocks),
        out_shape=jax.ShapeDtypeStruct(heads.shape, jnp.bfloat16),
        in_specs=[
            pl.BlockSpec(memory_space=pltpu.SMEM),
            pl.BlockSpec(memory_space=pltpu.VMEM),
        ],
        out_specs=pl.BlockSpec(memory_space=pltpu.VMEM),
        scratch_shapes=[
            pltpu.VMEM((key_total, 2 * DH, BLK), jnp.float32),
            pltpu.VMEM((blocks, groups, BLK, GROUP * BLK), jnp.float32),
            pltpu.VMEM((blocks, groups, BLK, GROUP * BLK), jnp.float32),
            pltpu.VMEM((blocks, groups, BLK, GROUP * BLK), jnp.bfloat16),
            pltpu.SMEM((blocks, key_total), jnp.int32),
            pltpu.SMEM((blocks,), jnp.int32),
        ],
        compiler_params=pltpu.CompilerParams(vmem_limit_bytes=16 << 20),
        cost_estimate=pl.CostEstimate(
            flops=tiles * 24 * BLK * BLK * DH, bytes_accessed=80 << 20,
            transcendentals=tiles * BLK * BLK,
        ),
        name="attend_heads",
    )(codes, heads)


def collect_kernel(
    n, n_row, res_ref, x_ref, wq_ref, wk_ref, wv_ref,
    att_ref, terms_in, part_in,
    inbox, terms_out, part_out,
    send_sem, recv_sem, term_send, term_recv, row_send, row_recv,
):
    me = lax.axis_index("col")
    my_row = lax.axis_index("row")
    meet([("col", n), ("row", n_row)])
    peers = [lax.rem(me + step, n) for step in range(1, n)]
    row_peers = [lax.rem(my_row + step, n_row) for step in range(1, n_row)]
    cols = part_out.shape[2]

    def res_copy(peer, slot):
        return pltpu.make_async_remote_copy(
            src_ref=res_ref.at[peer], dst_ref=inbox.at[slot], send_sem=send_sem.at[peer],
            recv_sem=recv_sem.at[slot], device_id={"col": peer}, device_id_type=MESH,
        )

    def term_copy(peer, slot):
        return pltpu.make_async_remote_copy(
            src_ref=terms_out.at[peer], dst_ref=terms_in.at[slot], send_sem=term_send.at[peer],
            recv_sem=term_recv.at[slot], device_id={"col": peer}, device_id_type=MESH,
        )

    def row_copy(peer, slot):
        return pltpu.make_async_remote_copy(
            src_ref=part_out.at[peer], dst_ref=part_in.at[slot], send_sem=row_send.at[peer],
            recv_sem=row_recv.at[slot], device_id={"row": peer}, device_id_type=MESH,
        )

    for peer in peers:
        res_copy(peer, me).start()
    inbox[me] = res_ref[me]
    rows = res_ref.shape[1]
    depth = x_ref.shape[3]
    chunk = depth // n
    turned = res_ref[...].reshape(n * rows, 4 * DH).T
    for peer in range(n):
        term = jnp.dot(
            turned,
            x_ref[:, :, :, peer * chunk : (peer + 1) * chunk].reshape(n * rows, chunk),
            preferred_element_type=jnp.float32,
        ).astype(jnp.bfloat16)
        terms_out[peer, :DH] = term[:DH]
        terms_out[peer, DH:] = term[2 * DH :]
    terms_in[me] = terms_out[me]
    for place, peer in enumerate(peers):
        res_copy(peer, peer).wait_recv()
        if place == len(peers) // 2:
            for target in peers:
                term_copy(target, me).start()

    def piece(which):
        return jnp.concatenate(
            [inbox[h, :, which * DH : (which + 1) * DH] for h in range(n)], axis=1
        )

    nt = (((1,), (1,)), ((), ()))
    grads = [piece(0), piece(2), piece(3)]
    weights = [wq_ref, wk_ref, wv_ref]
    for r in range(n_row):
        span = slice(r * cols, (r + 1) * cols)
        part = jnp.zeros((rows, cols), jnp.float32)
        for grad, weight in zip(grads, weights):
            part = part + lax.dot_general(
                grad, weight[span, :], nt, preferred_element_type=jnp.float32
            )
        part_out[r] = part.astype(jnp.bfloat16)
    for peer in row_peers:
        row_copy(peer, my_row).start()
    att_ref[...] = piece(1)
    for peer in peers:
        term_copy(peer, peer).wait_recv()
    part_in[my_row] = part_out[my_row]
    for peer in row_peers:
        row_copy(peer, peer).wait_recv()
    for peer in peers:
        res_copy(peer, me).wait_send()
        term_copy(peer, me).wait_send()
    for peer in row_peers:
        row_copy(peer, my_row).wait_send()


def finish_kernel(
    n, n_row, att_in, terms, parts, att_ref, node_ref, qg_ref, kg_ref, vg_ref,
    node_buf, grad_buf, sem,
):
    copies = [pltpu.make_async_copy(att_in, att_ref, sem.at[0])]
    copies[0].start()
    total = parts[0].astype(jnp.float32)
    for r in range(1, n_row):
        total = total + parts[r].astype(jnp.float32)
    node_buf[...] = total
    copies.append(pltpu.make_async_copy(node_buf, node_ref, sem.at[1]))
    copies[1].start()
    for which, ref in enumerate((qg_ref, kg_ref, vg_ref)):
        for h in range(0, n, 2):
            pair = jnp.concatenate(
                [
                    terms[h, which * DH : (which + 1) * DH],
                    terms[h + 1, which * DH : (which + 1) * DH],
                ],
                axis=0,
            )
            grad_buf[which, :, h * DH : (h + 2) * DH] = pair.astype(jnp.float32).T
        copies.append(pltpu.make_async_copy(grad_buf.at[which], ref, sem.at[2 + which]))
        copies[-1].start()
    for copy in copies:
        copy.wait()


def collect_grads(res, x_all, query_weight, key_weight, value_weight, n, n_row):
    rows = res.shape[1]
    depth = x_all.shape[3]
    cols = depth // n_row
    chunk = depth // n
    head_cols = n * DH
    vmem = pl.BlockSpec(memory_space=pltpu.VMEM)
    hbm = pl.BlockSpec(memory_space=pltpu.HBM)
    dma = pltpu.SemaphoreType.DMA
    att, terms, parts = pl.pallas_call(
        functools.partial(collect_kernel, n, n_row),
        out_shape=(
            jax.ShapeDtypeStruct((rows, head_cols), jnp.bfloat16),
            jax.ShapeDtypeStruct((n, 3 * DH, chunk), jnp.bfloat16),
            jax.ShapeDtypeStruct((n_row, rows, cols), jnp.bfloat16),
        ),
        in_specs=[vmem] * 5,
        out_specs=(vmem,) * 3,
        scratch_shapes=[
            pltpu.VMEM(res.shape, jnp.bfloat16),
            pltpu.VMEM((n, 3 * DH, chunk), jnp.bfloat16),
            pltpu.VMEM((n_row, rows, cols), jnp.bfloat16),
            dma((n,)), dma((n,)), dma((n,)), dma((n,)), dma((n_row,)), dma((n_row,)),
        ],
        compiler_params=pltpu.CompilerParams(
            collective_id=1, has_side_effects=True, vmem_limit_bytes=20 << 20
        ),
        name="collect_grads",
    )(res, x_all, query_weight, key_weight, value_weight)
    return pl.pallas_call(
        functools.partial(finish_kernel, n, n_row),
        out_shape=(
            jax.ShapeDtypeStruct((rows, head_cols), jnp.bfloat16),
            jax.ShapeDtypeStruct((rows, cols), jnp.float32),
            jax.ShapeDtypeStruct((chunk, head_cols), jnp.float32),
            jax.ShapeDtypeStruct((chunk, head_cols), jnp.float32),
            jax.ShapeDtypeStruct((chunk, head_cols), jnp.float32),
        ),
        in_specs=[vmem] * 3,
        out_specs=(hbm,) * 5,
        scratch_shapes=[
            pltpu.VMEM((rows, cols), jnp.float32),
            pltpu.VMEM((3, chunk, head_cols), jnp.float32),
            dma((5,)),
        ],
        compiler_params=pltpu.CompilerParams(vmem_limit_bytes=16 << 20),
        name="finish",
    )(att, terms, parts)


def per_device_heads(
    n, n_row, node_states, query_weight, key_weight, value_weight, output_grad, pair_list, pair_count
):
    blocks = node_states.shape[0] // BLK
    slots = pair_list.shape[1]
    listed = jnp.pad(pair_list[0].T, ((0, 0), (0, BLK - slots)))
    total = jnp.broadcast_to(pair_count[0], (6, BLK))
    codes = jnp.concatenate([listed, total], axis=0)
    heads, codes_all, x_all = spread(
        node_states, query_weight, key_weight, value_weight, output_grad, codes, n
    )
    res = attend(heads, codes_all, n, blocks)
    return collect_grads(res, x_all, query_weight, key_weight, value_weight, n, n_row)


def per_device(mesh, *arrays):
    n, n_row = mesh.shape["col"], mesh.shape["row"]
    node_states, query_weight, pair_list = arrays[0], arrays[1], arrays[5]
    blocks = node_states.shape[0] // BLK
    one_head_each = query_weight.shape[1] == n * DH and n % 2 == 0 and n_row == 2
    tiled = (n * blocks) % GROUP == 0 and pair_list.shape[1] <= BLK
    lanes = node_states.shape[1] % (n * BLK) == 0 and node_states.shape[1] % (n_row * BLK) == 0
    if one_head_each and tiled and lanes:
        return per_device_heads(n, n_row, *arrays)
    return per_device_slots(*arrays)


def solution(mesh):
    return jax.shard_map(
        functools.partial(per_device, mesh),
        mesh=mesh,
        in_specs=(
            P(("groups", "col"), None),
            P(None, "row"),
            P(None, "row"),
            P(None, "row"),
            P(("groups", "col"), "row"),
            P(("groups", "col"), None, None),
            P(("groups", "col")),
        ),
        out_specs=(
            P(("groups", "col"), "row"),
            P(("groups", "col"), "row"),
            P(("groups", "col"), "row"),
            P(("groups", "col"), "row"),
            P(("groups", "col"), "row"),
        ),
        check_vma=False,
    )
```
